32 devices in a mesh: section: 2 (over x), gy: 4 (over y, core), gx: 4 (over z).
Axes of the slice: x: 2, y: 2, z: 4, core: 2. Of those that a mesh axis runs over, the one named last changes fastest.
Arguments:
- images: bfloat16 [2, 128, 256, 128], P('section', 'gy', 'gx'), may hold values from -6 to 6
- first_kernel: bfloat16 [3, 3, 128, 128], replicated, may hold values from -0.1875 to 0.1875
- projection: bfloat16 [128, 256], replicated, may hold values from -0.5 to 0.5
- second_kernel: bfloat16 [3, 3, 256, 256], replicated, may hold values from -0.125 to 0.125
- cotangent: bfloat16 [2, 64, 128, 256], P('section', 'gy', 'gx'), may hold values from -0.625 to 0.625
Outputs:
- features: bfloat16 [2, 64, 128, 256], P('section', 'gy', 'gx')
- grad_first: float32 [3, 3, 128, 128], replicated
- grad_projection: float32 [128, 256], replicated
- grad_second: float32 [3, 3, 256, 256], replicated
The draws below stay inside these ranges and needn't reach their ends.
All inputs are finite; a program needn't handle non-finite values.
Results may differ from the reference program's by a relative error of at most 0.014.
Values may be sent and summed in bfloat16 or wider, within the bound.
No kernel may reach another device: no remote copies, remote signals or barrier semaphores. Data moves between devices by JAX's collectives and lax.ppermute only.
A program may use at most 64 MiB of HBM per device.

```python
import jax
import jax.numpy as jnp

CHANNELS = 128
CHANNELS_WIDE = 256
HEIGHT = 128
WIDTH = 256
HALF_HEIGHT = 64
HALF_WIDTH = 128


def block_scale(rng, shape, cuts, smallest, high):
    gain = 1.0
    for position, shards_of in cuts:
        draws = jax.random.uniform(jax.random.fold_in(jax.random.fold_in(rng, 6), position), (shards_of,), jnp.float32, smallest / len(cuts), high / len(cuts))
        gain = gain * jnp.repeat(jnp.exp(draws), shape[position] // shards_of).reshape((-1,) + (1,) * (len(shape) - 1 - position))
    return gain


def scatter_about(rng, dims, scale, reach, split=(), kind=jnp.bfloat16):
    level = block_scale(rng, dims, split, -0.22, 0.18) if split else 1.0
    result = jax.random.normal(rng, dims, jnp.float32) * scale * level
    return jnp.minimum(jnp.maximum(result, -reach), reach).astype(kind)


def setup_inputs(seed: int = 0) -> dict:
    seeds = jax.random.split(jax.random.key(seed), 6)
    return {
        "images": scatter_about(seeds[0], (2, HEIGHT, WIDTH, CHANNELS), 1.0, 6.0, ((0, 2), (1, 4), (2, 4))),
        "first_kernel": scatter_about(seeds[1], (3, 3, CHANNELS, CHANNELS), (9 * CHANNELS) ** -0.5, 0.1875),
        "projection": scatter_about(seeds[2], (CHANNELS, CHANNELS_WIDE), CHANNELS ** -0.5, 0.5),
        "second_kernel": scatter_about(seeds[3], (3, 3, CHANNELS_WIDE, CHANNELS_WIDE), (9 * CHANNELS_WIDE) ** -0.5, 0.125),
        "cotangent": scatter_about(seeds[4], (2, HALF_HEIGHT, HALF_WIDTH, CHANNELS_WIDE), (10.0 * (2 * HEIGHT * WIDTH) ** -0.5), 0.625, ((0, 2), (1, 4), (2, 4))),
    }


def silu_slope(values):
    sigma = jax.nn.sigmoid(values)
    return sigma * (1.0 + values * (1.0 - sigma))


def product(left, right):
    return jnp.dot(left.astype(jnp.float32), right.astype(jnp.float32))


def pad_field(field):
    return jnp.pad(field, ((1, 1), (1, 1), (0, 0)))


def conv_forward(padded, kernel, row_count, col_count):
    total = jnp.zeros((row_count * col_count, kernel.shape[3]), jnp.float32)
    for row_tap in range(3):
        for col_tap in range(3):
            piece = padded[row_tap:row_tap + row_count, col_tap:col_tap + col_count].reshape(row_count * col_count, padded.shape[2])
            total = total + product(piece, kernel[row_tap, col_tap])
    return total


def conv_slopes(padded, slope, row_count, col_count):
    pieces = []
    for row_tap in range(3):
        for col_tap in range(3):
            piece = padded[row_tap:row_tap + row_count, col_tap:col_tap + col_count].reshape(row_count * col_count, padded.shape[2])
            pieces.append(product(piece.T, slope))
    return jnp.stack(pieces).reshape(3, 3, padded.shape[2], slope.shape[1])


def conv_back(padded, kernel, row_count, col_count):
    total = jnp.zeros((row_count * col_count, kernel.shape[2]), jnp.float32)
    for row_tap in range(3):
        for col_tap in range(3):
            piece = padded[2 - row_tap:2 - row_tap + row_count, 2 - col_tap:2 - col_tap + col_count].reshape(row_count * col_count, padded.shape[2])
            total = total + product(piece, kernel[row_tap, col_tap].T)
    return total


def reference(images, first_kernel, projection, second_kernel, cotangent):
    outputs = []
    grad_first = jnp.zeros((3, 3, CHANNELS, CHANNELS), jnp.float32)
    grad_projection = jnp.zeros((CHANNELS, CHANNELS_WIDE), jnp.float32)
    grad_second = jnp.zeros((3, 3, CHANNELS_WIDE, CHANNELS_WIDE), jnp.float32)
    for source in range(2):
        padded_in = pad_field(images[source])
        before_one = conv_forward(padded_in, first_kernel, HEIGHT, WIDTH)
        hidden = jax.nn.silu(before_one).astype(jnp.bfloat16).reshape(HEIGHT, WIDTH, CHANNELS)
        pooled = (hidden.astype(jnp.float32).reshape(HALF_HEIGHT, 2, HALF_WIDTH, 2, CHANNELS).sum(axis=(1, 3)) * 0.25).astype(jnp.bfloat16)
        flat_pool = pooled.reshape(HALF_HEIGHT * HALF_WIDTH, CHANNELS)
        middle = product(flat_pool, projection).astype(jnp.bfloat16)
        padded_mid = pad_field(middle.reshape(HALF_HEIGHT, HALF_WIDTH, CHANNELS_WIDE))
        before_two = conv_forward(padded_mid, second_kernel, HALF_HEIGHT, HALF_WIDTH)
        outputs.append(jax.nn.silu(before_two).astype(jnp.bfloat16).reshape(HALF_HEIGHT, HALF_WIDTH, CHANNELS_WIDE))
        upstream = cotangent[1 - source].astype(jnp.float32).reshape(HALF_HEIGHT * HALF_WIDTH, CHANNELS_WIDE)
        slope_two = (upstream * silu_slope(before_two)).astype(jnp.bfloat16)
        grad_second = grad_second + conv_slopes(padded_mid, slope_two, HALF_HEIGHT, HALF_WIDTH)
        padded_slope = pad_field(slope_two.reshape(HALF_HEIGHT, HALF_WIDTH, CHANNELS_WIDE))
        middle_slope = conv_back(padded_slope, second_kernel, HALF_HEIGHT, HALF_WIDTH).astype(jnp.bfloat16)
        grad_projection = grad_projection + product(flat_pool.T, middle_slope)
        pooled_slope = product(middle_slope, projection.T).astype(jnp.bfloat16).reshape(HALF_HEIGHT, HALF_WIDTH, CHANNELS)
        spread = jnp.broadcast_to((pooled_slope.astype(jnp.float32) * 0.25)[:, None, :, None, :], (HALF_HEIGHT, 2, HALF_WIDTH, 2, CHANNELS)).reshape(HEIGHT * WIDTH, CHANNELS)
        slope_one = (spread * silu_slope(before_one)).astype(jnp.bfloat16)
        grad_first = grad_first + conv_slopes(padded_in, slope_one, HEIGHT, WIDTH)
    features = jnp.stack([outputs[1], outputs[0]])
    return features, grad_first, grad_projection, grad_second
```

```python
import jax
import jax.numpy as jnp
from jax import lax
from jax.sharding import PartitionSpec as P


GY = ("gy_hi", "core")


def padded_2(array, sides, width):
    for axis, dim in sides:
        size, length = (lax.axis_size(axis), array.shape[dim])
        up = [(i, (i + 1) % size) for i in range(size - 1)]
        down = [(j, i) for i, j in up]
        last = lax.slice_in_dim(array, length - width, length, axis=dim)
        initial = lax.slice_in_dim(array, 0, width, axis=dim)
        before = lax.ppermute(last, axis, up)
        after = lax.ppermute(initial, axis, down)
        array = jnp.concatenate([before, array, after], axis=dim)
    return array


def from_partner(block, axis, bit):
    count = lax.axis_size(axis)
    route = []
    for low in range(count):
        high = low | 1 << bit
        if high != low and high < count:
            route += [(low, high), (high, low)]
    return lax.ppermute(block, axis, route)


def silu_slope(values):
    sigma = jax.nn.sigmoid(values)
    return sigma * (1.0 + values * (1.0 - sigma))


def conv_forward(padded, kernel, row_count, col_count):
    total = jnp.zeros((row_count * col_count, kernel.shape[3]), jnp.float32)
    for row_tap in range(3):
        for col_tap in range(3):
            piece = padded[row_tap : row_tap + row_count, col_tap : col_tap + col_count].reshape(
                row_count * col_count, padded.shape[2]
            )
            total = total + jnp.dot(
                piece, kernel[row_tap, col_tap], preferred_element_type=jnp.float32
            )
    return total


def conv_slopes(padded, slope, row_count, col_count):
    pieces = []
    for row_tap in range(3):
        for col_tap in range(3):
            piece = padded[row_tap : row_tap + row_count, col_tap : col_tap + col_count].reshape(
                row_count * col_count, padded.shape[2]
            )
            pieces.append(jnp.einsum("pc,pd->cd", piece, slope, preferred_element_type=jnp.float32))
    return jnp.stack(pieces).reshape(3, 3, padded.shape[2], slope.shape[1])


def conv_back(padded, kernel, row_count, col_count):
    total = jnp.zeros((row_count * col_count, kernel.shape[2]), jnp.float32)
    for row_tap in range(3):
        for col_tap in range(3):
            piece = padded[
                2 - row_tap : 2 - row_tap + row_count, 2 - col_tap : 2 - col_tap + col_count
            ].reshape(row_count * col_count, padded.shape[2])
            total = total + jnp.einsum(
                "pd,cd->pc", piece, kernel[row_tap, col_tap], preferred_element_type=jnp.float32
            )
    return total


def first_forward(tile, first_kernel):
    row_count, col_count, channels = tile.shape
    padded = padded_2(tile, ((GY, 0), ("gx", 1)), 1)
    before = conv_forward(padded, first_kernel, row_count, col_count)
    hidden = jax.nn.silu(before).astype(jnp.bfloat16).reshape(row_count, col_count, channels)
    pooled = (
        hidden.astype(jnp.float32)
        .reshape(row_count // 2, 2, col_count // 2, 2, channels)
        .sum(axis=(1, 3))
        * 0.25
    ).astype(jnp.bfloat16)
    return (padded, before, pooled)


def project(pooled, projection):
    half_rows, half_cols, channels = pooled.shape
    flat = jnp.dot(
        pooled.reshape(half_rows * half_cols, channels),
        projection,
        preferred_element_type=jnp.float32,
    )
    return flat.astype(jnp.bfloat16).reshape(half_rows, half_cols, projection.shape[1])


def second_pass(middle, second_kernel, upstream):
    half_rows, half_cols, wide = middle.shape
    padded = padded_2(middle, ((GY, 0), ("gx", 1)), 1)
    before = conv_forward(padded, second_kernel, half_rows, half_cols)
    output = jax.nn.silu(before).astype(jnp.bfloat16).reshape(half_rows, half_cols, wide)
    flat_up = upstream.reshape(half_rows * half_cols, wide).astype(jnp.float32)
    slope = (flat_up * silu_slope(before)).astype(jnp.bfloat16)
    kernel_grad = conv_slopes(padded, slope, half_rows, half_cols)
    slope_padded = padded_2(slope.reshape(half_rows, half_cols, wide), ((GY, 0), ("gx", 1)), 1)
    back = conv_back(slope_padded, second_kernel, half_rows, half_cols).astype(jnp.bfloat16)
    return (output, kernel_grad, back.reshape(half_rows, half_cols, wide))


def projection_back(pooled, back, projection):
    half_rows, half_cols, channels = pooled.shape
    flat_pool = pooled.reshape(half_rows * half_cols, channels)
    flat_back = back.reshape(half_rows * half_cols, back.shape[2])
    grad = jnp.einsum("pc,pd->cd", flat_pool, flat_back, preferred_element_type=jnp.float32)
    pooled_slope = jnp.einsum(
        "pd,cd->pc", flat_back, projection, preferred_element_type=jnp.float32
    )
    return (grad, pooled_slope.astype(jnp.bfloat16).reshape(half_rows, half_cols, channels))


def first_back(padded, before, pooled_slope):
    half_rows, half_cols, channels = pooled_slope.shape
    spread = jnp.broadcast_to(
        (pooled_slope.astype(jnp.float32) * 0.25)[:, None, :, None, :],
        (half_rows, 2, half_cols, 2, channels),
    )
    spread = spread.reshape(4 * half_rows * half_cols, channels)
    slope = (spread * silu_slope(before)).astype(jnp.bfloat16)
    return conv_slopes(padded, slope, 2 * half_rows, 2 * half_cols)


def swap_pairs(block, axis):
    return lax.ppermute(block, axis, [(0, 1), (1, 0)])


def reduce_all(first, proj, second):
    plane, line = ("section", "gy_hi"), "gx"
    planes = lax.axis_size("section") * lax.axis_size("gy_hi")
    lines = lax.axis_size(line)
    wide = proj.shape[1]
    flat_first = first.reshape(-1, first.shape[3])
    fold = wide // first.shape[3]
    seg = flat_first.shape[0] // fold
    folded = jnp.concatenate([flat_first[i * seg : (i + 1) * seg] for i in range(fold)], axis=1)
    flat_second = second.reshape(-1, wide)
    rows = [folded.shape[0], proj.shape[0], flat_second.shape[0]]
    total = sum(rows)
    unit = 2 * planes * lines * 16
    padded = -(-total // unit) * unit
    flat = jnp.concatenate(
        [flat_second, proj, folded, jnp.zeros((padded - total, wide), jnp.float32)], axis=0
    )
    half = padded // 2
    core = lax.axis_index("core")
    low, high = flat[:half], flat[half:]
    mine = jnp.where(core == 0, low, high)
    other = jnp.where(core == 0, high, low).astype(jnp.bfloat16)
    summed = mine + swap_pairs(other, "core").astype(jnp.float32)
    for axes, count in ((plane, planes), (line, lines)):
        parts = summed.astype(jnp.bfloat16).reshape(count, summed.shape[0] // count, wide)
        parts = lax.all_to_all(parts, axes, 0, 0, tiled=True)
        summed = parts.astype(jnp.float32).sum(axis=0)
    whole = summed.astype(jnp.bfloat16)
    for axes, count in ((line, lines), (plane, planes)):
        parts = jnp.broadcast_to(whole[None], (count,) + whole.shape)
        whole = lax.all_to_all(parts, axes, 0, 0, tiled=True).reshape(-1, wide)
    theirs = swap_pairs(whole, "core")
    low = jnp.where(core == 0, whole, theirs)
    high = jnp.where(core == 0, theirs, whole)
    flat = jnp.concatenate([low, high], axis=0).astype(jnp.float32)
    second = flat[: rows[2]].reshape(second.shape)
    proj = flat[rows[2] : rows[2] + rows[1]]
    folded = flat[rows[2] + rows[1] : total]
    width = first.shape[3]
    first = jnp.concatenate(
        [folded[:, i * width : (i + 1) * width] for i in range(fold)], axis=0
    ).reshape(first.shape)
    return first, proj, second


def per_device(images, first_kernel, projection, second_kernel, cotangent):
    padded, before, pooled = first_forward(images[0], first_kernel)
    upstream = from_partner(cotangent[0], "section", 0)
    middle = project(pooled, projection)
    output, grad_second, back = second_pass(middle, second_kernel, upstream)
    grad_projection, pooled_slope = projection_back(pooled, back, projection)
    output = from_partner(output, "section", 0)
    grad_first = first_back(padded, before, pooled_slope)
    grad_first, grad_projection, grad_second = reduce_all(
        grad_first, grad_projection, grad_second
    )
    return (output[None], grad_first, grad_projection, grad_second)


def solution(mesh):
    shape = dict(mesh.shape)
    grid = mesh.devices.reshape(shape["section"], shape["gy"] // 2, 2, shape["gx"])
    split = jax.sharding.Mesh(grid, ("section", "gy_hi", "core", "gx"))
    tiles = P("section", ("gy_hi", "core"), "gx", None)
    return jax.shard_map(
        per_device,
        mesh=split,
        in_specs=(tiles, P(), P(), P(), tiles),
        out_specs=(tiles, P(), P(), P()),
        check_vma=False,
    )
```

```python
import jax
import jax.numpy as jnp
from jax import lax
from jax.sharding import PartitionSpec as P


GY = ("gy_hi", "core")


def silu_slope(values):
    sigma = jax.nn.sigmoid(values)
    return sigma * (1.0 + values * (1.0 - sigma))


DIMS = ("NHWC", "HWIO", "NHWC")


def conv(padded, kernel):
    return lax.conv_general_dilated(
        padded[None], kernel, (1, 1), "VALID", dimension_numbers=DIMS,
        preferred_element_type=jnp.float32,
    )[0]


def conv_back(padded, kernel):
    return conv(padded, jnp.swapaxes(kernel[::-1, ::-1], 2, 3))


def conv_slopes(padded, slope):
    return lax.conv_general_dilated(
        padded[None], slope[None], (1, 1), "VALID",
        dimension_numbers=("CHWN", "IHWO", "HWNC"), preferred_element_type=jnp.float32,
    )


def shifted(last, initial, axis):
    size = lax.axis_size(axis)
    up = [(i, i + 1) for i in range(size - 1)]
    down = [(j, i) for i, j in up]
    return lax.ppermute(last, axis, up), lax.ppermute(initial, axis, down)


def halo(tile, other, reach):
    rows, cols, channels = tile.shape

    def pack(a, b):
        return jnp.concatenate([a.reshape(-1, channels), b.reshape(-1, channels)], axis=0)

    before, after = shifted(
        pack(tile[rows - reach :], other[-1:]), pack(tile[:reach], other[:1]), GY
    )

    def opened(flat, shape, other_shape):
        size = shape[0] * shape[1]
        return flat[:size].reshape(shape), flat[size:].reshape(other_shape)

    shape, other_shape = (reach, cols, channels), (1,) + other.shape[1:]
    t_before, o_before = opened(before, shape, other_shape)
    t_after, o_after = opened(after, shape, other_shape)
    tile = jnp.concatenate([t_before, tile, t_after], axis=0)
    other = jnp.concatenate([o_before, other, o_after], axis=0)
    before, after = shifted(
        pack(tile[:, cols - reach :], other[:, -1:]), pack(tile[:, :reach], other[:, :1]), "gx"
    )
    shape, other_shape = (tile.shape[0], reach, channels), (other.shape[0], 1, other.shape[2])
    t_before, o_before = opened(before, shape, other_shape)
    t_after, o_after = opened(after, shape, other_shape)
    tile = jnp.concatenate([t_before, tile, t_after], axis=1)
    ring = [o_before, o_after, other[:1], other[-1:]]
    return tile, ring


def inside(count, margin, axis):
    where = lax.axis_index(axis) * count + lax.iota(jnp.int32, count + 2 * margin) - margin
    return (where >= 0) & (where < count * lax.axis_size(axis))


def swap_pairs(block, axis):
    return lax.ppermute(block, axis, [(0, 1), (1, 0)])


def reduce_all(first, proj, second):
    plane, line = ("section", "gy_hi"), "gx"
    planes = lax.axis_size("section") * lax.axis_size("gy_hi")
    lines = lax.axis_size(line)
    wide = proj.shape[1]
    flat_first = first.reshape(-1, first.shape[3])
    fold = wide // first.shape[3]
    seg = flat_first.shape[0] // fold
    folded = jnp.concatenate([flat_first[i * seg : (i + 1) * seg] for i in range(fold)], axis=1)
    flat_second = second.reshape(-1, wide)
    rows = [folded.shape[0], proj.shape[0], flat_second.shape[0]]
    total = sum(rows)
    unit = 2 * planes * lines * 16
    padded = -(-total // unit) * unit
    flat = jnp.concatenate(
        [flat_second, proj, folded, jnp.zeros((padded - total, wide), jnp.float32)], axis=0
    )
    half = padded // 2
    core = lax.axis_index("core")
    low, high = flat[:half], flat[half:]
    mine = jnp.where(core == 0, low, high)
    other = jnp.where(core == 0, high, low).astype(jnp.bfloat16)
    summed = mine + swap_pairs(other, "core").astype(jnp.float32)
    for axes, count in ((plane, planes), (line, lines)):
        parts = summed.astype(jnp.bfloat16).reshape(count, summed.shape[0] // count, wide)
        parts = lax.all_to_all(parts, axes, 0, 0, tiled=True)
        summed = parts.astype(jnp.float32).sum(axis=0)
    whole = summed.astype(jnp.bfloat16)
    for axes, count in ((line, lines), (plane, planes)):
        parts = jnp.broadcast_to(whole[None], (count,) + whole.shape)
        whole = lax.all_to_all(parts, axes, 0, 0, tiled=True).reshape(-1, wide)
    theirs = swap_pairs(whole, "core")
    low = jnp.where(core == 0, whole, theirs)
    high = jnp.where(core == 0, theirs, whole)
    flat = jnp.concatenate([low, high], axis=0).astype(jnp.float32)
    second = flat[: rows[2]].reshape(second.shape)
    proj = flat[rows[2] : rows[2] + rows[1]]
    folded = flat[rows[2] + rows[1] : total]
    width = first.shape[3]
    first = jnp.concatenate(
        [folded[:, i * width : (i + 1) * width] for i in range(fold)], axis=0
    ).reshape(first.shape)
    return first, proj, second


def per_device(images, first_kernel, projection, second_kernel, cotangent):
    image, upstream = images[0], cotangent[0]
    rows, cols, channels = image.shape
    half_rows, half_cols, wide = upstream.shape
    theirs = swap_pairs(upstream, "section")
    padded, ring = halo(image, upstream, 5)
    flat = jnp.concatenate([piece.reshape(-1, wide) for piece in ring], axis=0)
    flat = swap_pairs(flat, "section")
    pieces, at = [], 0
    for piece in ring:
        count = piece.shape[0] * piece.shape[1]
        pieces.append(flat[at : at + count].reshape(piece.shape))
        at += count
    left, right, top, bottom = pieces
    theirs = jnp.concatenate([top, theirs, bottom], axis=0)
    theirs = jnp.concatenate([left, theirs, right], axis=1)

    before = conv(padded, first_kernel)
    hidden = jax.nn.silu(before).astype(jnp.bfloat16)
    pooled = (
        hidden.astype(jnp.float32)
        .reshape(half_rows + 4, 2, half_cols + 4, 2, channels)
        .sum(axis=(1, 3))
        * 0.25
    ).astype(jnp.bfloat16)
    middle = jnp.einsum("ijc,cd->ijd", pooled, projection, preferred_element_type=jnp.float32)
    mask = inside(half_rows, 2, GY)[:, None] & inside(half_cols, 2, "gx")[None, :]
    middle = jnp.where(mask[:, :, None], middle, 0.0).astype(jnp.bfloat16)
    before_two = conv(middle, second_kernel)
    output = jax.nn.silu(before_two[1:-1, 1:-1]).astype(jnp.bfloat16)
    output = swap_pairs(output, "section")
    slope_two = (theirs.astype(jnp.float32) * silu_slope(before_two)).astype(jnp.bfloat16)
    own_slope = slope_two[1:-1, 1:-1]
    grad_second = conv_slopes(middle[1:-1, 1:-1], own_slope)
    back = conv_back(slope_two, second_kernel).astype(jnp.bfloat16)
    grad_projection = jnp.einsum(
        "ijc,ijd->cd", pooled[2:-2, 2:-2], back, preferred_element_type=jnp.float32
    )
    pooled_slope = jnp.einsum(
        "ijd,cd->ijc", back, projection, preferred_element_type=jnp.float32
    ).astype(jnp.bfloat16)
    spread = jnp.broadcast_to(
        (pooled_slope.astype(jnp.float32) * 0.25)[:, None, :, None, :],
        (half_rows, 2, half_cols, 2, channels),
    ).reshape(rows, cols, channels)
    slope = (spread * silu_slope(before[4:-4, 4:-4])).astype(jnp.bfloat16)
    grad_first = conv_slopes(padded[4:-4, 4:-4], slope)
    output, grad_first, grad_projection, grad_second = lax.optimization_barrier(
        (output, grad_first, grad_projection, grad_second)
    )
    grad_first, grad_projection, grad_second = reduce_all(
        grad_first, grad_projection, grad_second
    )
    return (output[None], grad_first, grad_projection, grad_second)


def solution(mesh):
    shape = dict(mesh.shape)
    grid = mesh.devices.reshape(shape["section"], shape["gy"] // 2, 2, shape["gx"])
    split = jax.sharding.Mesh(grid, ("section", "gy_hi", "core", "gx"))
    tiles = P("section", ("gy_hi", "core"), "gx", None)
    return jax.shard_map(
        per_device,
        mesh=split,
        in_specs=(tiles, P(), P(), P(), tiles),
        out_specs=(tiles, P(), P(), P()),
        check_vma=False,
    )
```

```python
import functools
import math

import jax
import jax.numpy as jnp
from jax import lax
from jax.experimental import pallas as pl
from jax.experimental.pallas import tpu as pltpu
from jax.sharding import PartitionSpec as P

F32, BF16 = jnp.float32, jnp.bfloat16
NT, TN = (((1,), (1,)), ((), ())), (((0,), (0,)), ((), ()))
SIDE, EDGE, REACH = 8, 48, 5
GY, GX = ("gy_hi", "core"), ("gx_hi", "gx_lo")
PLANE = ("section", "gy_hi", "gx_lo")


def dot(left, right):
    return jnp.dot(left, right, preferred_element_type=F32)


def sloped(values):
    sigma = 1.0 / (1.0 + jnp.exp(-values))
    return sigma * (1.0 + values * (1.0 - sigma))


def silu(values):
    return values / (1.0 + jnp.exp(-values))


def spread_taps(value, out, lanes):
    cols = value.shape[1]
    out[..., 0:lanes] = pltpu.roll(value, 1, 1).astype(BF16)
    out[..., lanes : 2 * lanes] = value.astype(BF16)
    out[..., 2 * lanes : 3 * lanes] = pltpu.roll(value, cols - 1, 1).astype(BF16)


def sides(even, odd, axes):
    place, first = lax.axis_index(axes), lax.axis_index(axes[1]) == 0
    even, odd = even.astype(F32), odd.astype(F32)
    lower, upper = jnp.where(first, odd, even), jnp.where(first, even, odd)
    lower = jnp.where(place == 0, 0.0, lower)
    return lower, jnp.where(place == lax.axis_size(axes) - 1, 0.0, upper)


def forward_kernel(
    tile, rows_even, rows_odd, cols_even, cols_odd, first_kernel, projection, second_kernel,
    features, taps_one, field_one, taps_mid, field_two, pool, weights_one, sums,
):
    rows, cols, lanes = tile.shape
    half_rows, half_cols, wide = features.shape
    pitch = cols + 2 * SIDE
    reach = rows_even.shape[0] - 1
    tall = rows + 2 * reach
    above, below = sides(rows_even[0:reach], rows_odd[0:reach], GY)
    body = jnp.concatenate([above, tile[...].astype(F32), below], axis=0)
    before, after = sides(cols_even[0 : tall * SIDE], cols_odd[0 : tall * SIDE], GX)
    before, after = [side.reshape(tall, SIDE, lanes) for side in (before, after)]
    full = jnp.concatenate([body, after, before], axis=1)
    spread_taps(full, taps_one, lanes)
    for row in range(4):
        at = row * 3 * lanes
        zero = jnp.zeros((3 * lanes, lanes), BF16)
        left = first_kernel[row].reshape(3 * lanes, lanes) if row < 3 else zero
        right = first_kernel[row - 1].reshape(3 * lanes, lanes) if row else zero
        weights_one[at : at + 3 * lanes, 0:lanes] = left
        weights_one[at : at + 3 * lanes, lanes : 2 * lanes] = right
    pairs = half_rows + 4
    step = 10 if pairs % 10 == 0 else pairs

    def first(index, carry):
        pair = index * step
        picked = [
            taps_one[pl.ds(2 * pair + row // 2 * 2, 2 * step)]
            .reshape(step, 2, pitch, 3 * lanes)[:, row % 2]
            .reshape(step * pitch, 3 * lanes)
            for row in range(4)
        ]
        value = dot(jnp.concatenate(picked, axis=1), weights_one[...])
        field_one[pl.ds(pair, step)] = value.reshape(step, pitch, 2 * lanes)
        hidden = silu(value).astype(BF16).astype(F32)
        at = pl.multiple_of(pair * pitch, 8)
        sums[pl.ds(at, step * pitch), :] = hidden[:, :lanes] + hidden[:, lanes:]
        return carry

    lax.fori_loop(0, pairs // step, first, 0)
    half_pitch = pitch // 2
    cells = pairs * half_pitch
    pooled = (
        0.25 * (sums[pl.ds(0, cells, stride=2), :] + sums[pl.ds(1, cells, stride=2), :])
    ).astype(BF16)
    own_pool = pooled.astype(F32).reshape(pairs, half_pitch, lanes)
    pool[...] = own_pool[2 : half_rows + 2, 0:half_cols].astype(BF16)
    middle = dot(pooled, projection[...]).reshape(pairs, half_pitch, wide)
    row = lax.broadcasted_iota(jnp.int32, middle.shape, 0)
    col = lax.broadcasted_iota(jnp.int32, middle.shape, 1)
    gy, gx = lax.axis_index(GY), lax.axis_index(GX)
    low = jnp.where(gy == 0, 2, 0)
    high = jnp.where(gy == lax.axis_size(GY) - 1, pairs - 2, pairs)
    right = jnp.where(gx == lax.axis_size(GX) - 1, half_cols, half_cols + SIDE // 2)
    left = jnp.where(gx == 0, half_pitch, half_cols + SIDE // 2)
    keep = (row >= low) & (row < high) & ((col < right) | (col >= left))
    middle = jnp.where(keep, middle, 0.0)
    middle = jnp.concatenate([middle, middle[:, half_pitch - 8 :]], axis=1)
    spread_taps(middle, taps_mid, wide)
    pitch_two = half_pitch + 8
    outs = half_rows + 2
    part = outs

    def second(index, carry):
        at = index * part
        picked = [
            taps_mid[pl.ds(at + row, part)].reshape(part * pitch_two, 3 * wide) for row in range(3)
        ]
        value = dot(
            jnp.concatenate(picked, axis=1), second_kernel[...].reshape(9 * wide, wide)
        )
        field_two[pl.ds(at, part)] = value.reshape(part, pitch_two, wide)
        return carry

    lax.fori_loop(0, outs // part, second, 0)
    features[...] = silu(field_two[1 : half_rows + 1, 0:half_cols]).astype(BF16)


def split_halves(flat, mine, other, chunk):
    half, core, flip = mine.shape[0], lax.axis_index("core"), lax.axis_index(GX[0])
    count = half // chunk if chunk else 1
    size = half // count
    for block in range(count):
        place = flip * (1 - 2 * (block % 2)) + block if chunk else 0
        at = pl.ds(block * size, size)
        for target, owner in ((mine, core), (other, 1 - core)):
            start = pl.multiple_of(owner * half + place * size, 64)
            target[at, :] = flat[pl.ds(start, size), :]


def backward_kernel(
    chunk, theirs, ring, taps_one, field_one, taps_mid, field_two, pool, projection, second_kernel,
    mine, other, cot, taps_slope, up, flat,
):
    half_rows, half_cols, wide = theirs.shape
    lanes = projection.shape[0]
    rows, cols, pitch = 2 * half_rows, 2 * half_cols, taps_one.shape[1]
    outs, pitch_two = field_two.shape[:2]
    cot[...] = jnp.zeros(cot.shape, F32)
    cot[1 : half_rows + 1, 0:half_cols] = theirs[...].astype(F32)
    top, bottom = sides(ring[0:cols], ring[cols : 2 * cols], GY)
    at = 2 * cols
    left, right = sides(ring[at : at + EDGE], ring[at + EDGE : at + 2 * EDGE], GX)
    for part in range(2):
        lane = slice(part * lanes, (part + 1) * lanes)
        at = part * half_cols
        cot[0, 0:half_cols, lane] = top[at : at + half_cols]
        cot[half_rows + 1, 0:half_cols, lane] = bottom[at : at + half_cols]
        at = part * (EDGE // 2)
        cot[:, pitch_two - 1 : pitch_two, lane] = left[at : at + outs].reshape(outs, 1, lanes)
        cot[:, half_cols : half_cols + 1, lane] = right[at : at + outs].reshape(outs, 1, lanes)
    slope_two = cot[...] * sloped(field_two[...])
    spread_taps(slope_two, taps_slope, wide)
    own = half_rows * half_cols
    own_slope = slope_two[1 : half_rows + 1, 0:half_cols].reshape(own, wide).astype(BF16)
    for row in range(3):
        window = taps_mid[row + 1 : row + 1 + half_rows, 0:half_cols].reshape(own, 3 * wide)
        grad = lax.dot_general(window, own_slope, TN, preferred_element_type=F32)
        for col in range(3):
            at = (row * 3 + col) * wide
            flat[at : at + wide, :] = grad[col * wide : (col + 1) * wide].astype(BF16)
    windows = [
        taps_slope[row : row + half_rows, 0:half_cols].reshape(own, 3 * wide) for row in range(3)
    ]
    kernels = [second_kernel[2 - row, 2 - col] for row in range(3) for col in range(3)]
    kernels = jnp.concatenate(kernels, axis=1)
    windows = jnp.concatenate(windows, axis=1)
    cut = own // 2
    back = [
        lax.dot_general(windows[at : at + cut], kernels, NT, preferred_element_type=F32)
        for at in (0, cut)
    ]
    back = jnp.concatenate(back, axis=0).astype(BF16)
    at = 9 * wide
    flat[at : at + lanes, :] = dot(pool[...].astype(F32).reshape(own, lanes).T.astype(BF16), back).astype(BF16)
    at += lanes
    down = lax.dot_general(back, projection[...], NT, preferred_element_type=F32)
    down = down.astype(BF16).astype(F32) * 0.25
    up[pl.ds(0, own, stride=2), :] = down
    up[pl.ds(1, own, stride=2), :] = down
    cells = 2 * own
    field = field_one[2 : half_rows + 2, 0:cols].reshape(cells, 2 * lanes)
    slope_one = jnp.concatenate([up[...], up[...]], axis=1) * sloped(field)
    slope_one = slope_one.astype(BF16)
    grads = []
    for row in range(4):
        start = REACH - 1 + row
        window = taps_one[start : start + rows].reshape(half_rows, 2, pitch, 3 * lanes)[:, 0, 0:cols]
        window = window.reshape(cells, 3 * lanes)
        grads.append(lax.dot_general(window, slope_one, TN, preferred_element_type=F32))
    for tap in range(9):
        row, col = tap // 3, tap % 3
        span = slice(col * lanes, (col + 1) * lanes)
        grad = grads[row][span, :lanes] + grads[row + 1][span, lanes:]
        top = at + (tap % 4) * lanes + (4 * lanes if tap == 8 else 0)
        side = lanes if 4 <= tap < 8 else 0
        flat[top : top + lanes, side : side + lanes] = grad.astype(BF16)
    top = at + 4 * lanes
    flat[top : top + lanes, lanes : 2 * lanes] = jnp.zeros((lanes, lanes), BF16)
    used = at + 5 * lanes
    total = flat.shape[0]
    if used < total:
        flat[used:total, :] = jnp.zeros((total - used, wide), BF16)
    split_halves(flat, mine, other, chunk)


def resident(*arrays):
    return [pltpu.with_memory_space_constraint(array, pltpu.VMEM) for array in arrays]


def forward(tile, halo, first_kernel, projection, second_kernel):
    rows, cols, lanes = tile.shape
    half_rows, half_cols, wide = rows // 2, cols // 2, projection.shape[1]
    pitch = cols + 2 * SIDE
    pitch_two = pitch // 2 + 8
    vmem = pl.BlockSpec(memory_space=pltpu.VMEM)
    return pl.pallas_call(
        forward_kernel,
        out_shape=(
            pltpu.VMEM((half_rows, half_cols, wide), BF16),
            pltpu.VMEM((rows + 2 * REACH, pitch, 3 * lanes), BF16),
            pltpu.VMEM((half_rows + 4, pitch, 2 * lanes), F32),
            pltpu.VMEM((half_rows + 4, pitch_two, 3 * wide), BF16),
            pltpu.VMEM((half_rows + 2, pitch_two, wide), F32),
            pltpu.VMEM((half_rows, half_cols, lanes), BF16),
        ),
        in_specs=[vmem] * 8,
        out_specs=(vmem,) * 6,
        scratch_shapes=[
            pltpu.VMEM((12 * lanes, 2 * lanes), BF16),
            pltpu.VMEM(((half_rows + 4) * pitch, lanes), F32),
        ],
        compiler_params=pltpu.CompilerParams(vmem_limit_bytes=20 << 20),
    )(
        *resident(tile, *halo, first_kernel, projection, second_kernel),
    )


def backward(theirs, ring, kept, projection, second_kernel, total, chunk):
    half_rows, half_cols, wide = theirs.shape
    outs, pitch_two = kept[3].shape[:2]
    lanes = projection.shape[0]
    vmem = pl.BlockSpec(memory_space=pltpu.VMEM)
    return pl.pallas_call(
        functools.partial(backward_kernel, chunk),
        out_shape=(
            pltpu.VMEM((total // 2, wide), BF16),
            pltpu.VMEM((total // 2, wide), BF16),
        ),
        in_specs=[vmem] * 9,
        out_specs=(vmem,) * 2,
        scratch_shapes=[
            pltpu.VMEM((outs, pitch_two, wide), F32),
            pltpu.VMEM((outs, pitch_two, 3 * wide), BF16),
            pltpu.VMEM((4 * half_rows * half_cols // 2, lanes), F32),
            pltpu.VMEM((total, wide), BF16),
        ],
        compiler_params=pltpu.CompilerParams(vmem_limit_bytes=24 << 20),
    )(*resident(theirs, ring, *kept, projection, second_kernel))


def unpack_half(own, chunk, source, grads, held, sent):
    first, projection, second = grads
    lanes, wide = projection.shape
    half, flip = source.shape[0], lax.axis_index(GX[0])
    low = lax.axis_index("core") == (0 if own else 1)
    piece = math.gcd(64, chunk) if chunk else lanes
    jobs = []

    def send(rows, side, target):
        at, inside = rows[0] % half, rows[0] < half
        slot = sent.at[len(jobs)]
        span = slice(at, at + rows[1])
        here = low if inside else jnp.logical_not(low)

        @pl.when(here)
        def _():
            for step in range(at, at + rows[1], piece):
                start = step
                if chunk:
                    start = step + flip * (1 - 2 * (step // chunk % 2)) * chunk
                    start = pl.multiple_of(start, piece)
                held[step : step + piece, side] = source[pl.ds(start, piece), side].astype(F32)
            pltpu.make_async_copy(held.at[span, side], target, slot).start()

        jobs.append((here, held.at[span, side], target, slot))

    whole = slice(0, wide)
    for tap in range(9):
        send((tap * wide, wide), whole, second.at[tap // 3, tap % 3])
    at = 9 * wide
    send((at, lanes), whole, projection)
    at += lanes
    for tap in range(9):
        top = at + (tap % 4) * lanes + (4 * lanes if tap == 8 else 0)
        side = lanes if 4 <= tap < 8 else 0
        send((top, lanes), slice(side, side + lanes), first.at[tap // 3, tap % 3])
    for here, origin, target, slot in jobs:

        @pl.when(here)
        def _(origin=origin, target=target, slot=slot):
            pltpu.make_async_copy(origin, target, slot).wait()


def unpack_own(chunk, source, first, projection, second, held, sent):
    unpack_half(True, chunk, source, (first, projection, second), held, sent)


def unpack_other(
    chunk, source, features, first_in, projection_in, second_in, output, first, projection, second,
    held, sent,
):
    copy = pltpu.make_async_copy(features, output, sent.at[19])
    copy.start()
    unpack_half(False, chunk, source, (first, projection, second), held, sent)
    copy.wait()


def unpack_call(kernel, chunk, arrays, outs, aliases):
    vmem, hbm = pl.BlockSpec(memory_space=pltpu.VMEM), pl.BlockSpec(memory_space=pl.ANY)
    resting = len(aliases)
    moving = resident(*arrays[: len(arrays) - resting])
    return pl.pallas_call(
        functools.partial(kernel, chunk),
        out_shape=outs,
        in_specs=[vmem] * len(moving) + [hbm] * resting,
        out_specs=(hbm,) * len(outs),
        scratch_shapes=[
            pltpu.VMEM(arrays[0].shape, F32),
            pltpu.SemaphoreType.DMA((20,)),
        ],
        input_output_aliases=aliases,
        compiler_params=pltpu.CompilerParams(vmem_limit_bytes=12 << 20),
    )(*moving, *arrays[len(arrays) - resting :])


def swap_pairs(block, axis):
    return lax.ppermute(block, axis, [(0, 1), (1, 0)])


def swap_neighbours(even, odd, axes, spare):
    size, others = lax.axis_size(axes), lax.axis_size(spare)
    near = [(i, i + 1) for i in range(0, size, 2)]
    far = [(i, i + 1) for i in range(1, size - 1, 2)]
    leading = spare == "gy_hi"

    def place(i, at):
        return at * size + i if leading else i * others + at

    far = [(place(i, at), place(j, at)) for i, j in far for at in range(others)]
    ends = [(i, at) for i in (0, size - 1) for at in range(0, others, 2)]
    far += [(place(i, at), place(i, at + 1)) for i, at in ends]
    names = (spare,) + axes if leading else axes + (spare,)

    def both(pairs):
        return [pair for i, j in pairs for pair in ((i, j), (j, i))]

    odd = lax.ppermute(odd, names, both(far))
    even = lax.ppermute(even, axes, both(near))
    return even, odd


def edges_kernel(
    image, upstream, rows_even, rows_odd, tile_even, tile_odd, strip_even, strip_odd, sent,
):
    rows, cols, lanes = image.shape
    half_rows, half_cols, _ = upstream.shape
    lower, left = lax.axis_index("core") == 0, lax.axis_index("gx_lo") == 0
    copies = []

    def send(source, target):
        copy = pltpu.make_async_copy(source, target, sent.at[len(copies)])
        copy.start()
        copies.append(copy)

    for target, at_end in ((rows_odd, ~lower), (rows_even, lower)):
        start = jnp.where(at_end, rows - REACH, 0)
        row = jnp.where(at_end, half_rows - 1, 0)
        send(image.at[pl.ds(start, REACH)], target.at[0:REACH])
        for part in range(2):
            send(
                upstream.at[row, :, part * lanes : (part + 1) * lanes],
                target.at[REACH, part * half_cols : (part + 1) * half_cols],
            )
    for target, strip, at_end in ((tile_odd, strip_odd, ~left), (tile_even, strip_even, left)):
        start = pl.multiple_of(jnp.where(at_end, cols - SIDE, 0), SIDE)
        cell = pl.multiple_of(jnp.where(at_end, half_cols - SIDE, 0), SIDE)
        send(image.at[:, pl.ds(start, SIDE)], target)
        send(upstream.at[:, pl.ds(cell, SIDE)], strip)
    for copy in copies:
        copy.wait()


def edges(image, upstream):
    hbm, vmem = pl.BlockSpec(memory_space=pl.ANY), pl.BlockSpec(memory_space=pltpu.VMEM)
    rows, cols, lanes = image.shape
    half_rows, _, wide = upstream.shape
    shapes = [(REACH + 1, cols, lanes), (rows, SIDE, lanes), (half_rows, SIDE, wide)]
    return pl.pallas_call(
        edges_kernel,
        out_shape=[pltpu.VMEM(shape, BF16) for shape in shapes for _ in range(2)],
        in_specs=[hbm, hbm],
        out_specs=[vmem] * 6,
        scratch_shapes=[pltpu.SemaphoreType.DMA((10,))],
        compiler_params=pltpu.CompilerParams(vmem_limit_bytes=4 << 20),
    )(*[pltpu.with_memory_space_constraint(array, pltpu.HBM) for array in (image, upstream)])


def columns_kernel(
    rows_even, rows_odd, tile_even, tile_odd, strip_even, strip_odd, even, odd, edge
):
    rows, side, lanes = tile_even.shape
    half_rows = strip_even.shape[0]
    cols = rows_even.shape[1]
    half_cols = cols // 2
    tall = rows + 2 * REACH
    left = lax.axis_index("gx_lo") == 0
    above, below = sides(rows_even[...], rows_odd[...], GY)
    for target, tile, strip, at_end in (
        (odd, tile_odd, strip_odd, ~left), (even, tile_even, strip_even, left),
    ):

        def near(block):
            return jnp.where(at_end, block[0:REACH, cols - side :], block[0:REACH, 0:side])

        body = jnp.concatenate([near(above), tile[...].astype(F32), near(below)], axis=0)
        target[0 : tall * side] = body.reshape(tall * side, lanes).astype(BF16)
        edge[...] = jnp.zeros(edge.shape, F32)
        cells = strip[...].astype(F32)
        cells = jnp.where(at_end, cells[:, side - 1], cells[:, 0])
        for part in range(2):
            at, first = part * (EDGE // 2), part * half_cols

            def corner(block):
                last = first + half_cols - 1
                low, high = block[REACH, first : first + 1], block[REACH, last : last + 1]
                return jnp.where(at_end, high, low)

            edge[at : at + 1] = corner(above)
            edge[at + 1 : at + half_rows + 1] = cells[:, part * lanes : (part + 1) * lanes]
            at += half_rows + 1
            edge[at : at + 1] = corner(below)
        target[tall * side : tall * side + EDGE] = edge[...].astype(BF16)


def fetch_kernel(*refs):
    count = len(refs) // 2
    sent = refs[-1]
    copies = [pltpu.make_async_copy(refs[i], refs[count + i], sent.at[i]) for i in range(count)]
    for copy in copies:
        copy.start()
    for copy in copies:
        copy.wait()


def fetch(*arrays):
    hbm, vmem = pl.BlockSpec(memory_space=pl.ANY), pl.BlockSpec(memory_space=pltpu.VMEM)
    return pl.pallas_call(
        fetch_kernel,
        out_shape=[pltpu.VMEM(array.shape, array.dtype) for array in arrays],
        in_specs=[hbm] * len(arrays),
        out_specs=[vmem] * len(arrays),
        scratch_shapes=[pltpu.SemaphoreType.DMA((len(arrays),))],
        compiler_params=pltpu.CompilerParams(vmem_limit_bytes=1 << 20),
    )(*[pltpu.with_memory_space_constraint(array, pltpu.HBM) for array in arrays])


def edge_columns(*arrays):
    vmem = pl.BlockSpec(memory_space=pltpu.VMEM)
    rows, side, lanes = arrays[2].shape
    shape = ((rows + 2 * REACH) * side + EDGE, lanes)
    return pl.pallas_call(
        columns_kernel,
        out_shape=(pltpu.VMEM(shape, BF16),) * 2,
        in_specs=[vmem] * 6,
        out_specs=(vmem,) * 2,
        scratch_shapes=[pltpu.VMEM((EDGE, lanes), F32)],
        compiler_params=pltpu.CompilerParams(vmem_limit_bytes=8 << 20),
    )(*resident(*arrays))


def scatter_sum(parts, axes):
    parts = lax.all_to_all(parts, axes, 0, 0, tiled=True)
    return parts.astype(F32).sum(axis=0).astype(BF16)


def gather(part, axes, count):
    parts = jnp.broadcast_to(part[None], (count,) + part.shape)
    return lax.all_to_all(parts, axes, 0, 0, tiled=True).reshape(-1, part.shape[1])


def per_device(images, first_kernel, projection, second_kernel, cotangent):
    image, upstream = images[0], cotangent[0]
    _, _, wide = upstream.shape
    _, _, lanes = image.shape
    rows_even, rows_odd, *strips = edges(image, upstream)
    rows_even, rows_odd = swap_neighbours(rows_even, rows_odd, GY, "gx_lo")
    packed = edge_columns(rows_even, rows_odd, *strips)
    cols_even, cols_odd = swap_neighbours(*packed, GX, "gy_hi")
    tile, *weights = fetch(image, first_kernel, projection, second_kernel)
    theirs = swap_pairs(upstream, "section")
    ring = [rows_even[REACH], rows_odd[REACH], cols_even[-EDGE:], cols_odd[-EDGE:]]
    ring = swap_pairs(jnp.concatenate(ring), "section")

    planes = lax.axis_size("section") * lax.axis_size("gy_hi") * lax.axis_size("gx_lo")
    lines = lax.axis_size("gx_hi")
    unit = 2 * planes * lines * 16
    total = -(-(9 * wide + 6 * lanes) // unit) * unit
    halo = (rows_even, rows_odd, cols_even, cols_odd)
    output, *kept = forward(tile, halo, *weights)
    output = swap_pairs(output, "section")
    chunk = total // 2 // planes if lines == 2 else 0
    mine, other = backward(theirs, ring, kept, *weights[1:], total, chunk)
    part = (mine.astype(F32) + swap_pairs(other, "core").astype(F32)).astype(BF16)
    part = scatter_sum(part.reshape(planes, -1, wide), PLANE)
    if lines == 2:
        pairs = [(0, 3), (1, 2), (2, 1), (3, 0)]
        theirs = lax.ppermute(part, GX, pairs)
        part = (part.astype(F32) + theirs.astype(F32)).astype(BF16)
    elif lines > 2:
        part = scatter_sum(part.reshape(lines, -1, wide), "gx_hi")
        part = gather(part, "gx_hi", lines)
    whole = gather(part, PLANE, planes)
    others = swap_pairs(whole, "core")
    shapes = (first_kernel.shape, projection.shape, second_kernel.shape)
    outs = tuple(jax.ShapeDtypeStruct(shape, F32) for shape in shapes)
    grads = unpack_call(unpack_own, chunk, (whole,), outs, {})
    outs = (jax.ShapeDtypeStruct(output.shape, BF16),) + outs
    output, *grads = unpack_call(
        unpack_other, chunk, (others, output, *grads), outs, {2: 1, 3: 2, 4: 3}
    )
    return (output[None], *grads)


def solution(mesh):
    shape = dict(mesh.shape)
    sizes = (shape["section"], shape["gy"] // 2, 2, shape["gx"] // 2, 2)
    names = ("section", "gy_hi", "core", "gx_hi", "gx_lo")
    split = jax.sharding.Mesh(mesh.devices.reshape(sizes), names)
    tiles = P("section", GY, GX, None)
    return jax.shard_map(
        per_device,
        mesh=split,
        in_specs=(tiles, P(), P(), P(), tiles),
        out_specs=(tiles, P(), P(), P()),
        check_vma=False,
    )
```

```python
import functools
import math

import jax
import jax.numpy as jnp
from jax import lax
from jax.experimental import pallas as pl
from jax.experimental.pallas import tpu as pltpu
from jax.sharding import PartitionSpec as P

F32, BF16 = jnp.float32, jnp.bfloat16
NT, TN = (((1,), (1,)), ((), ())), (((0,), (0,)), ((), ()))
SIDE, EDGE, REACH = 8, 48, 5
GY, GX = ("gy_hi", "core"), ("gx_hi", "gx_lo")
PLANE = ("section", "gy_hi", "gx_lo")


def dot(left, right):
    return jnp.dot(left, right, preferred_element_type=F32)


def sloped(values):
    sigma = 1.0 / (1.0 + jnp.exp(-values))
    return sigma * (1.0 + values * (1.0 - sigma))


def silu(values):
    return values / (1.0 + jnp.exp(-values))


def spread_taps(value, out, lanes):
    cols = value.shape[1]
    out[..., 0:lanes] = pltpu.roll(value, 1, 1).astype(BF16)
    out[..., lanes : 2 * lanes] = value.astype(BF16)
    out[..., 2 * lanes : 3 * lanes] = pltpu.roll(value, cols - 1, 1).astype(BF16)


def sides(even, odd, axes):
    place, first = lax.axis_index(axes), lax.axis_index(axes[1]) == 0
    even, odd = even.astype(F32), odd.astype(F32)
    lower, upper = jnp.where(first, odd, even), jnp.where(first, even, odd)
    lower = jnp.where(place == 0, 0.0, lower)
    return lower, jnp.where(place == lax.axis_size(axes) - 1, 0.0, upper)


def forward_kernel(
    tile, rows_even, rows_odd, cols_even, cols_odd, first_kernel, projection, second_kernel,
    features, taps_one, field_one, taps_mid, field_two, pool, weights_one, sums,
):
    rows, cols, lanes = tile.shape
    half_rows, half_cols, wide = features.shape
    pitch = cols + 2 * SIDE
    reach = rows_even.shape[0] - 1
    tall = rows + 2 * reach
    above, below = sides(rows_even[0:reach], rows_odd[0:reach], GY)
    body = jnp.concatenate([above, tile[...].astype(F32), below], axis=0)
    before, after = sides(cols_even[0 : tall * SIDE], cols_odd[0 : tall * SIDE], GX)
    before, after = [side.reshape(tall, SIDE, lanes) for side in (before, after)]
    full = jnp.concatenate([body, after, before], axis=1)
    spread_taps(full, taps_one, lanes)
    for row in range(4):
        at = row * 3 * lanes
        zero = jnp.zeros((3 * lanes, lanes), BF16)
        left = first_kernel[row].reshape(3 * lanes, lanes) if row < 3 else zero
        right = first_kernel[row - 1].reshape(3 * lanes, lanes) if row else zero
        weights_one[at : at + 3 * lanes, 0:lanes] = left
        weights_one[at : at + 3 * lanes, lanes : 2 * lanes] = right
    pairs = half_rows + 4
    step = 10 if pairs % 10 == 0 else pairs

    def first(index, carry):
        pair = index * step
        picked = [
            taps_one[pl.ds(2 * pair + row // 2 * 2, 2 * step)]
            .reshape(step, 2, pitch, 3 * lanes)[:, row % 2]
            .reshape(step * pitch, 3 * lanes)
            for row in range(4)
        ]
        value = dot(jnp.concatenate(picked, axis=1), weights_one[...])
        field_one[pl.ds(pair, step)] = value.reshape(step, pitch, 2 * lanes)
        hidden = silu(value).astype(BF16).astype(F32)
        at = pl.multiple_of(pair * pitch, 8)
        sums[pl.ds(at, step * pitch), :] = hidden[:, :lanes] + hidden[:, lanes:]
        return carry

    lax.fori_loop(0, pairs // step, first, 0)
    half_pitch = pitch // 2
    cells = pairs * half_pitch
    pooled = (
        0.25 * (sums[pl.ds(0, cells, stride=2), :] + sums[pl.ds(1, cells, stride=2), :])
    ).astype(BF16)
    own_pool = pooled.astype(F32).reshape(pairs, half_pitch, lanes)
    pool[...] = own_pool[2 : half_rows + 2, 0:half_cols].astype(BF16)
    middle = dot(pooled, projection[...]).reshape(pairs, half_pitch, wide)
    row = lax.broadcasted_iota(jnp.int32, middle.shape, 0)
    col = lax.broadcasted_iota(jnp.int32, middle.shape, 1)
    gy, gx = lax.axis_index(GY), lax.axis_index(GX)
    low = jnp.where(gy == 0, 2, 0)
    high = jnp.where(gy == lax.axis_size(GY) - 1, pairs - 2, pairs)
    right = jnp.where(gx == lax.axis_size(GX) - 1, half_cols, half_cols + SIDE // 2)
    left = jnp.where(gx == 0, half_pitch, half_cols + SIDE // 2)
    keep = (row >= low) & (row < high) & ((col < right) | (col >= left))
    middle = jnp.where(keep, middle, 0.0)
    spread_taps(middle, taps_mid, wide)
    pitch_two = half_pitch
    outs = half_rows + 2
    part = outs

    def second(index, carry):
        at = index * part
        picked = [
            taps_mid[pl.ds(at + row, part)].reshape(part * pitch_two, 3 * wide) for row in range(3)
        ]
        value = dot(
            jnp.concatenate(picked, axis=1), second_kernel[...].reshape(9 * wide, wide)
        )
        field_two[pl.ds(at, part)] = value.reshape(part, pitch_two, wide)
        return carry

    lax.fori_loop(0, outs // part, second, 0)
    features[...] = silu(field_two[1 : half_rows + 1, 0:half_cols]).astype(BF16)


def split_halves(flat, mine, other, chunk):
    half, core, flip = mine.shape[0], lax.axis_index("core"), lax.axis_index(GX[0])
    count = half // chunk if chunk else 1
    size = half // count
    for block in range(count):
        place = flip * (1 - 2 * (block % 2)) + block if chunk else 0
        at = pl.ds(block * size, size)
        for target, owner in ((mine, core), (other, 1 - core)):
            start = pl.multiple_of(owner * half + place * size, 64)
            target[at, :] = flat[pl.ds(start, size), :]


def backward_kernel(
    chunk, theirs, ring, taps_one, field_one, taps_mid, field_two, pool, projection, second_kernel,
    mine, other, cot, taps_slope, up, flat,
):
    half_rows, half_cols, wide = theirs.shape
    lanes = projection.shape[0]
    rows, cols, pitch = 2 * half_rows, 2 * half_cols, taps_one.shape[1]
    outs, pitch_two = field_two.shape[:2]
    cot[...] = jnp.zeros(cot.shape, F32)
    cot[1 : half_rows + 1, 0:half_cols] = theirs[...].astype(F32)
    top, bottom = sides(ring[0:cols], ring[cols : 2 * cols], GY)
    at = 2 * cols
    left, right = sides(ring[at : at + EDGE], ring[at + EDGE : at + 2 * EDGE], GX)
    for part in range(2):
        lane = slice(part * lanes, (part + 1) * lanes)
        at = part * half_cols
        cot[0, 0:half_cols, lane] = top[at : at + half_cols]
        cot[half_rows + 1, 0:half_cols, lane] = bottom[at : at + half_cols]
        at = part * (EDGE // 2)
        cot[:, pitch_two - 1 : pitch_two, lane] = left[at : at + outs].reshape(outs, 1, lanes)
        cot[:, half_cols : half_cols + 1, lane] = right[at : at + outs].reshape(outs, 1, lanes)
    slope_two = cot[...] * sloped(field_two[...])
    spread_taps(slope_two, taps_slope, wide)
    own = half_rows * half_cols
    own_slope = slope_two[1 : half_rows + 1, 0:half_cols].reshape(own, wide).astype(BF16)
    for row in range(3):
        window = taps_mid[row + 1 : row + 1 + half_rows, 0:half_cols].reshape(own, 3 * wide)
        grad = lax.dot_general(window, own_slope, TN, preferred_element_type=F32)
        for col in range(3):
            at = (row * 3 + col) * wide
            flat[at : at + wide, :] = grad[col * wide : (col + 1) * wide].astype(BF16)
    windows = [
        taps_slope[row : row + half_rows, 0:half_cols].reshape(own, 3 * wide) for row in range(3)
    ]
    kernels = [second_kernel[2 - row, 2 - col] for row in range(3) for col in range(3)]
    kernels = jnp.concatenate(kernels, axis=1)
    windows = jnp.concatenate(windows, axis=1)
    cut = own // 2
    back = [
        lax.dot_general(windows[at : at + cut], kernels, NT, preferred_element_type=F32)
        for at in (0, cut)
    ]
    back = jnp.concatenate(back, axis=0).astype(BF16)
    at = 9 * wide
    flat[at : at + lanes, :] = dot(pool[...].astype(F32).reshape(own, lanes).T.astype(BF16), back).astype(BF16)
    at += lanes
    down = lax.dot_general(back, projection[...], NT, preferred_element_type=F32)
    down = down.astype(BF16).astype(F32) * 0.25
    up[pl.ds(0, own, stride=2), :] = down
    up[pl.ds(1, own, stride=2), :] = down
    cells = 2 * own
    field = field_one[2 : half_rows + 2, 0:cols].reshape(cells, 2 * lanes)
    slope_one = jnp.concatenate([up[...], up[...]], axis=1) * sloped(field)
    slope_one = slope_one.astype(BF16)
    grads = []
    for row in range(4):
        start = REACH - 1 + row
        window = taps_one[start : start + rows].reshape(half_rows, 2, pitch, 3 * lanes)[:, 0, 0:cols]
        window = window.reshape(cells, 3 * lanes)
        grads.append(lax.dot_general(window, slope_one, TN, preferred_element_type=F32))
    for tap in range(9):
        row, col = tap // 3, tap % 3
        span = slice(col * lanes, (col + 1) * lanes)
        grad = grads[row][span, :lanes] + grads[row + 1][span, lanes:]
        top = at + (tap % 4) * lanes + (4 * lanes if tap == 8 else 0)
        side = lanes if 4 <= tap < 8 else 0
        flat[top : top + lanes, side : side + lanes] = grad.astype(BF16)
    top = at + 4 * lanes
    flat[top : top + lanes, lanes : 2 * lanes] = jnp.zeros((lanes, lanes), BF16)
    used = at + 5 * lanes
    total = flat.shape[0]
    if used < total:
        flat[used:total, :] = jnp.zeros((total - used, wide), BF16)
    split_halves(flat, mine, other, chunk)


def resident(*arrays):
    return [pltpu.with_memory_space_constraint(array, pltpu.VMEM) for array in arrays]


def forward(tile, halo, first_kernel, projection, second_kernel):
    rows, cols, lanes = tile.shape
    half_rows, half_cols, wide = rows // 2, cols // 2, projection.shape[1]
    pitch = cols + 2 * SIDE
    pitch_two = pitch // 2
    vmem = pl.BlockSpec(memory_space=pltpu.VMEM)
    return pl.pallas_call(
        forward_kernel,
        out_shape=(
            pltpu.VMEM((half_rows, half_cols, wide), BF16),
            pltpu.VMEM((rows + 2 * REACH, pitch, 3 * lanes), BF16),
            pltpu.VMEM((half_rows + 4, pitch, 2 * lanes), F32),
            pltpu.VMEM((half_rows + 4, pitch_two, 3 * wide), BF16),
            pltpu.VMEM((half_rows + 2, pitch_two, wide), F32),
            pltpu.VMEM((half_rows, half_cols, lanes), BF16),
        ),
        in_specs=[vmem] * 8,
        out_specs=(vmem,) * 6,
        scratch_shapes=[
            pltpu.VMEM((12 * lanes, 2 * lanes), BF16),
            pltpu.VMEM(((half_rows + 4) * pitch, lanes), F32),
        ],
        compiler_params=pltpu.CompilerParams(vmem_limit_bytes=20 << 20),
    )(
        *resident(tile, *halo, first_kernel, projection, second_kernel),
    )


def backward(theirs, ring, kept, projection, second_kernel, total, chunk):
    half_rows, half_cols, wide = theirs.shape
    outs, pitch_two = kept[3].shape[:2]
    lanes = projection.shape[0]
    vmem = pl.BlockSpec(memory_space=pltpu.VMEM)
    return pl.pallas_call(
        functools.partial(backward_kernel, chunk),
        out_shape=(
            pltpu.VMEM((total // 2, wide), BF16),
            pltpu.VMEM((total // 2, wide), BF16),
        ),
        in_specs=[vmem] * 9,
        out_specs=(vmem,) * 2,
        scratch_shapes=[
            pltpu.VMEM((outs, pitch_two, wide), F32),
            pltpu.VMEM((outs, pitch_two, 3 * wide), BF16),
            pltpu.VMEM((4 * half_rows * half_cols // 2, lanes), F32),
            pltpu.VMEM((total, wide), BF16),
        ],
        compiler_params=pltpu.CompilerParams(vmem_limit_bytes=24 << 20),
    )(*resident(theirs, ring, *kept, projection, second_kernel))


def unpack_half(own, chunk, source, grads, held, sent):
    first, projection, second = grads
    lanes, wide = projection.shape
    half, flip = source.shape[0], lax.axis_index(GX[0])
    low = lax.axis_index("core") == (0 if own else 1)
    piece = math.gcd(64, chunk) if chunk else lanes
    jobs = []

    def send(rows, side, target):
        at, inside = rows[0] % half, rows[0] < half
        slot = sent.at[len(jobs)]
        span = slice(at, at + rows[1])
        here = low if inside else jnp.logical_not(low)

        @pl.when(here)
        def _():
            for step in range(at, at + rows[1], piece):
                start = step
                if chunk:
                    start = step + flip * (1 - 2 * (step // chunk % 2)) * chunk
                    start = pl.multiple_of(start, piece)
                held[step : step + piece, side] = source[pl.ds(start, piece), side].astype(F32)
            pltpu.make_async_copy(held.at[span, side], target, slot).start()

        jobs.append((here, held.at[span, side], target, slot))

    whole = slice(0, wide)
    for tap in range(9):
        send((tap * wide, wide), whole, second.at[tap // 3, tap % 3])
    at = 9 * wide
    send((at, lanes), whole, projection)
    at += lanes
    for tap in range(9):
        top = at + (tap % 4) * lanes + (4 * lanes if tap == 8 else 0)
        side = lanes if 4 <= tap < 8 else 0
        send((top, lanes), slice(side, side + lanes), first.at[tap // 3, tap % 3])
    for here, origin, target, slot in jobs:

        @pl.when(here)
        def _(origin=origin, target=target, slot=slot):
            pltpu.make_async_copy(origin, target, slot).wait()


def unpack_own(chunk, source, first, projection, second, held, sent):
    unpack_half(True, chunk, source, (first, projection, second), held, sent)


def unpack_other(
    chunk, source, features, first_in, projection_in, second_in, output, first, projection, second,
    held, sent,
):
    copy = pltpu.make_async_copy(features, output, sent.at[19])
    copy.start()
    unpack_half(False, chunk, source, (first, projection, second), held, sent)
    copy.wait()


def unpack_call(kernel, chunk, arrays, outs, aliases):
    vmem, hbm = pl.BlockSpec(memory_space=pltpu.VMEM), pl.BlockSpec(memory_space=pl.ANY)
    resting = len(aliases)
    moving = resident(*arrays[: len(arrays) - resting])
    return pl.pallas_call(
        functools.partial(kernel, chunk),
        out_shape=outs,
        in_specs=[vmem] * len(moving) + [hbm] * resting,
        out_specs=(hbm,) * len(outs),
        scratch_shapes=[
            pltpu.VMEM(arrays[0].shape, F32),
            pltpu.SemaphoreType.DMA((20,)),
        ],
        input_output_aliases=aliases,
        compiler_params=pltpu.CompilerParams(vmem_limit_bytes=12 << 20),
    )(*moving, *arrays[len(arrays) - resting :])


def swap_pairs(block, axis):
    return lax.ppermute(block, axis, [(0, 1), (1, 0)])


def swap_neighbours(even, odd, axes, spare):
    size, others = lax.axis_size(axes), lax.axis_size(spare)
    near = [(i, i + 1) for i in range(0, size, 2)]
    far = [(i, i + 1) for i in range(1, size - 1, 2)]
    leading = spare == "gy_hi"

    def place(i, at):
        return at * size + i if leading else i * others + at

    far = [(place(i, at), place(j, at)) for i, j in far for at in range(others)]
    ends = [(i, at) for i in (0, size - 1) for at in range(0, others, 2)]
    far += [(place(i, at), place(i, at + 1)) for i, at in ends]
    names = (spare,) + axes if leading else axes + (spare,)

    def both(pairs):
        return [pair for i, j in pairs for pair in ((i, j), (j, i))]

    odd = lax.ppermute(odd, names, both(far))
    even = lax.ppermute(even, axes, both(near))
    return even, odd


def rows_kernel(image, upstream, rows_even, rows_odd, sent):
    rows, _, lanes = image.shape
    half_rows, half_cols, _ = upstream.shape
    lower = lax.axis_index("core") == 0
    copies = []

    def send(source, target):
        copy = pltpu.make_async_copy(source, target, sent.at[len(copies)])
        copy.start()
        copies.append(copy)

    for target, at_end in ((rows_odd, ~lower), (rows_even, lower)):
        start = jnp.where(at_end, rows - REACH, 0)
        row = jnp.where(at_end, half_rows - 1, 0)
        send(image.at[pl.ds(start, REACH)], target.at[0:REACH])
        for part in range(2):
            send(
                upstream.at[row, :, part * lanes : (part + 1) * lanes],
                target.at[REACH, part * half_cols : (part + 1) * half_cols],
            )
    for copy in copies:
        copy.wait()


def strips_kernel(image, upstream, tile_even, tile_odd, strip_even, strip_odd, sent):
    _, cols, _ = image.shape
    _, half_cols, _ = upstream.shape
    left = lax.axis_index("gx_lo") == 0
    copies = []

    def send(source, target):
        copy = pltpu.make_async_copy(source, target, sent.at[len(copies)])
        copy.start()
        copies.append(copy)

    for target, strip, at_end in ((tile_odd, strip_odd, ~left), (tile_even, strip_even, left)):
        start = pl.multiple_of(jnp.where(at_end, cols - SIDE, 0), SIDE)
        cell = pl.multiple_of(jnp.where(at_end, half_cols - SIDE, 0), SIDE)
        send(image.at[:, pl.ds(start, SIDE)], target)
        send(upstream.at[:, pl.ds(cell, SIDE)], strip)
    for copy in copies:
        copy.wait()


def cut(kernel, shapes, image, upstream):
    hbm, vmem = pl.BlockSpec(memory_space=pl.ANY), pl.BlockSpec(memory_space=pltpu.VMEM)
    return pl.pallas_call(
        kernel,
        out_shape=[pltpu.VMEM(shape, BF16) for shape in shapes for _ in range(2)],
        in_specs=[hbm, hbm],
        out_specs=[vmem] * (2 * len(shapes)),
        scratch_shapes=[pltpu.SemaphoreType.DMA((6,))],
        compiler_params=pltpu.CompilerParams(vmem_limit_bytes=4 << 20),
    )(*[pltpu.with_memory_space_constraint(array, pltpu.HBM) for array in (image, upstream)])


def columns_kernel(
    rows_even, rows_odd, tile_even, tile_odd, strip_even, strip_odd, even, odd, edge
):
    rows, side, lanes = tile_even.shape
    half_rows = strip_even.shape[0]
    cols = rows_even.shape[1]
    half_cols = cols // 2
    tall = rows + 2 * REACH
    left = lax.axis_index("gx_lo") == 0
    above, below = sides(rows_even[...], rows_odd[...], GY)
    for target, tile, strip, at_end in (
        (odd, tile_odd, strip_odd, ~left), (even, tile_even, strip_even, left),
    ):

        def near(block):
            return jnp.where(at_end, block[0:REACH, cols - side :], block[0:REACH, 0:side])

        body = jnp.concatenate([near(above), tile[...].astype(F32), near(below)], axis=0)
        target[0 : tall * side] = body.reshape(tall * side, lanes).astype(BF16)
        edge[...] = jnp.zeros(edge.shape, F32)
        cells = strip[...].astype(F32)
        cells = jnp.where(at_end, cells[:, side - 1], cells[:, 0])
        for part in range(2):
            at, first = part * (EDGE // 2), part * half_cols

            def corner(block):
                last = first + half_cols - 1
                low, high = block[REACH, first : first + 1], block[REACH, last : last + 1]
                return jnp.where(at_end, high, low)

            edge[at : at + 1] = corner(above)
            edge[at + 1 : at + half_rows + 1] = cells[:, part * lanes : (part + 1) * lanes]
            at += half_rows + 1
            edge[at : at + 1] = corner(below)
        target[tall * side : tall * side + EDGE] = edge[...].astype(BF16)


def fetch_kernel(*refs):
    count = len(refs) // 2
    sent = refs[-1]
    copies = [pltpu.make_async_copy(refs[i], refs[count + i], sent.at[i]) for i in range(count)]
    for copy in copies:
        copy.start()
    for copy in copies:
        copy.wait()


def fetch(*arrays):
    hbm, vmem = pl.BlockSpec(memory_space=pl.ANY), pl.BlockSpec(memory_space=pltpu.VMEM)
    return pl.pallas_call(
        fetch_kernel,
        out_shape=[pltpu.VMEM(array.shape, array.dtype) for array in arrays],
        in_specs=[hbm] * len(arrays),
        out_specs=[vmem] * len(arrays),
        scratch_shapes=[pltpu.SemaphoreType.DMA((len(arrays),))],
        compiler_params=pltpu.CompilerParams(vmem_limit_bytes=1 << 20),
    )(*[pltpu.with_memory_space_constraint(array, pltpu.HBM) for array in arrays])


def edge_columns(*arrays):
    vmem = pl.BlockSpec(memory_space=pltpu.VMEM)
    rows, side, lanes = arrays[2].shape
    shape = ((rows + 2 * REACH) * side + EDGE, lanes)
    return pl.pallas_call(
        columns_kernel,
        out_shape=(pltpu.VMEM(shape, BF16),) * 2,
        in_specs=[vmem] * 6,
        out_specs=(vmem,) * 2,
        scratch_shapes=[pltpu.VMEM((EDGE, lanes), F32)],
        compiler_params=pltpu.CompilerParams(vmem_limit_bytes=8 << 20),
    )(*resident(*arrays))


def scatter_sum(parts, axes):
    parts = lax.all_to_all(parts, axes, 0, 0, tiled=True)
    return parts.astype(F32).sum(axis=0).astype(BF16)


def gather(part, axes, count):
    parts = jnp.broadcast_to(part[None], (count,) + part.shape)
    return lax.all_to_all(parts, axes, 0, 0, tiled=True).reshape(-1, part.shape[1])


def per_device(images, first_kernel, projection, second_kernel, cotangent):
    image, upstream = images[0], cotangent[0]
    half_rows, _, wide = upstream.shape
    rows, cols, lanes = image.shape
    rows_even, rows_odd = cut(rows_kernel, [(REACH + 1, cols, lanes)], image, upstream)
    shapes = [(rows, SIDE, lanes), (half_rows, SIDE, wide)]
    strips = cut(strips_kernel, shapes, image, upstream)
    rows_even, rows_odd = swap_neighbours(rows_even, rows_odd, GY, "gx_lo")
    packed = edge_columns(rows_even, rows_odd, *strips)
    cols_even, cols_odd = swap_neighbours(*packed, GX, "gy_hi")
    tile, *weights = fetch(image, first_kernel, projection, second_kernel)
    theirs = swap_pairs(upstream, "section")
    ring = [rows_even[REACH], rows_odd[REACH], cols_even[-EDGE:], cols_odd[-EDGE:]]
    ring = swap_pairs(jnp.concatenate(ring), "section")

    planes = lax.axis_size("section") * lax.axis_size("gy_hi") * lax.axis_size("gx_lo")
    lines = lax.axis_size("gx_hi")
    unit = 2 * planes * lines * 16
    total = -(-(9 * wide + 6 * lanes) // unit) * unit
    halo = (rows_even, rows_odd, cols_even, cols_odd)
    output, *kept = forward(tile, halo, *weights)
    output = swap_pairs(output, "section")
    chunk = total // 2 // planes if lines == 2 else 0
    mine, other = backward(theirs, ring, kept, *weights[1:], total, chunk)
    part = (mine.astype(F32) + swap_pairs(other, "core").astype(F32)).astype(BF16)
    part = scatter_sum(part.reshape(planes, -1, wide), PLANE)
    if lines == 2:
        pairs = [(0, 3), (1, 2), (2, 1), (3, 0)]
        theirs = lax.ppermute(part, GX, pairs)
        part = (part.astype(F32) + theirs.astype(F32)).astype(BF16)
    elif lines > 2:
        part = scatter_sum(part.reshape(lines, -1, wide), "gx_hi")
        part = gather(part, "gx_hi", lines)
    whole = gather(part, PLANE, planes)
    others = swap_pairs(whole, "core")
    shapes = (first_kernel.shape, projection.shape, second_kernel.shape)
    outs = tuple(jax.ShapeDtypeStruct(shape, F32) for shape in shapes)
    grads = unpack_call(unpack_own, chunk, (whole,), outs, {})
    outs = (jax.ShapeDtypeStruct(output.shape, BF16),) + outs
    output, *grads = unpack_call(
        unpack_other, chunk, (others, output, *grads), outs, {2: 1, 3: 2, 4: 3}
    )
    return (output[None], *grads)


def solution(mesh):
    shape = dict(mesh.shape)
    sizes = (shape["section"], shape["gy"] // 2, 2, shape["gx"] // 2, 2)
    names = ("section", "gy_hi", "core", "gx_hi", "gx_lo")
    split = jax.sharding.Mesh(mesh.devices.reshape(sizes), names)
    tiles = P("section", GY, GX, None)
    return jax.shard_map(
        per_device,
        mesh=split,
        in_specs=(tiles, P(), P(), P(), tiles),
        out_specs=(tiles, P(), P(), P()),
        check_vma=False,
    )
```

```python
import functools
import math

import jax
import jax.numpy as jnp
from jax import lax
from jax.experimental import pallas as pl
from jax.experimental.pallas import tpu as pltpu
from jax.sharding import PartitionSpec as P

F32, BF16 = jnp.float32, jnp.bfloat16
NT, TN = (((1,), (1,)), ((), ())), (((0,), (0,)), ((), ()))
SIDE, EDGE, REACH = 8, 48, 5
GY, GX = ("gy_hi", "core"), ("gx_hi", "gx_lo")
PLANE = ("section", "gy_hi", "gx_lo")


def dot(left, right):
    return jnp.dot(left, right, preferred_element_type=F32)


def sloped(values):
    sigma = 1.0 / (1.0 + jnp.exp(-values))
    return sigma * (1.0 + values * (1.0 - sigma))


def silu(values):
    return values / (1.0 + jnp.exp(-values))


def spread_taps(value, out, lanes):
    cols = value.shape[1]
    out[..., 0:lanes] = pltpu.roll(value, 1, 1).astype(BF16)
    out[..., lanes : 2 * lanes] = value.astype(BF16)
    out[..., 2 * lanes : 3 * lanes] = pltpu.roll(value, cols - 1, 1).astype(BF16)


def sides(even, odd, axes):
    place, first = lax.axis_index(axes), lax.axis_index(axes[1]) == 0
    even, odd = even.astype(F32), odd.astype(F32)
    lower, upper = jnp.where(first, odd, even), jnp.where(first, even, odd)
    lower = jnp.where(place == 0, 0.0, lower)
    return lower, jnp.where(place == lax.axis_size(axes) - 1, 0.0, upper)


def forward_kernel(
    tile, rows_even, rows_odd, cols_even, cols_odd, first_kernel, projection, second_kernel,
    features, taps_one, field_one, taps_mid, field_two, pool, weights_one, sums,
):
    rows, cols, lanes = tile.shape
    half_rows, half_cols, wide = features.shape
    pitch = cols + 2 * SIDE
    reach = rows_even.shape[0] - 1
    tall = rows + 2 * reach
    above, below = sides(rows_even[0:reach], rows_odd[0:reach], GY)
    body = jnp.concatenate([above, tile[...].astype(F32), below], axis=0)
    before, after = sides(cols_even[0 : tall * SIDE], cols_odd[0 : tall * SIDE], GX)
    before, after = [side.reshape(tall, SIDE, lanes) for side in (before, after)]
    full = jnp.concatenate([body, after, before], axis=1)
    spread_taps(full, taps_one, lanes)
    for row in range(4):
        at = row * 3 * lanes
        zero = jnp.zeros((3 * lanes, lanes), BF16)
        left = first_kernel[row].reshape(3 * lanes, lanes) if row < 3 else zero
        right = first_kernel[row - 1].reshape(3 * lanes, lanes) if row else zero
        weights_one[at : at + 3 * lanes, 0:lanes] = left
        weights_one[at : at + 3 * lanes, lanes : 2 * lanes] = right
    pairs = half_rows + 4
    step = 10 if pairs % 10 == 0 else pairs

    def first(index, carry):
        pair = index * step
        picked = [
            taps_one[pl.ds(2 * pair + row // 2 * 2, 2 * step)]
            .reshape(step, 2, pitch, 3 * lanes)[:, row % 2]
            .reshape(step * pitch, 3 * lanes)
            for row in range(4)
        ]
        value = dot(jnp.concatenate(picked, axis=1), weights_one[...])
        field_one[pl.ds(pair, step)] = value.reshape(step, pitch, 2 * lanes)
        hidden = silu(value).astype(BF16).astype(F32)
        at = pl.multiple_of(pair * pitch, 8)
        sums[pl.ds(at, step * pitch), :] = hidden[:, :lanes] + hidden[:, lanes:]
        return carry

    lax.fori_loop(0, pairs // step, first, 0)
    half_pitch = pitch // 2
    cells = pairs * half_pitch
    pooled = (
        0.25 * (sums[pl.ds(0, cells, stride=2), :] + sums[pl.ds(1, cells, stride=2), :])
    ).astype(BF16)
    own_pool = pooled.astype(F32).reshape(pairs, half_pitch, lanes)
    pool[...] = own_pool[2 : half_rows + 2, 0:half_cols].astype(BF16)
    middle = dot(pooled, projection[...]).reshape(pairs, half_pitch, wide)
    row = lax.broadcasted_iota(jnp.int32, middle.shape, 0)
    col = lax.broadcasted_iota(jnp.int32, middle.shape, 1)
    gy, gx = lax.axis_index(GY), lax.axis_index(GX)
    low = jnp.where(gy == 0, 2, 0)
    high = jnp.where(gy == lax.axis_size(GY) - 1, pairs - 2, pairs)
    right = jnp.where(gx == lax.axis_size(GX) - 1, half_cols, half_cols + SIDE // 2)
    left = jnp.where(gx == 0, half_pitch, half_cols + SIDE // 2)
    keep = (row >= low) & (row < high) & ((col < right) | (col >= left))
    middle = jnp.where(keep, middle, 0.0)
    spread_taps(middle, taps_mid, wide)
    pitch_two = half_pitch
    outs = half_rows + 2
    part = outs

    def second(index, carry):
        at = index * part
        picked = [
            taps_mid[pl.ds(at + row, part)].reshape(part * pitch_two, 3 * wide) for row in range(3)
        ]
        value = dot(
            jnp.concatenate(picked, axis=1), second_kernel[...].reshape(9 * wide, wide)
        )
        field_two[pl.ds(at, part)] = value.reshape(part, pitch_two, wide)
        return carry

    lax.fori_loop(0, outs // part, second, 0)
    features[...] = silu(field_two[1 : half_rows + 1, 0:half_cols]).astype(BF16)


def split_halves(flat, mine, other, chunk):
    half, core, flip = mine.shape[0], lax.axis_index("core"), lax.axis_index(GX[0])
    count = half // chunk if chunk else 1
    size = half // count
    for block in range(count):
        place = flip * (1 - 2 * (block % 2)) + block if chunk else 0
        at = pl.ds(block * size, size)
        for target, owner in ((mine, core), (other, 1 - core)):
            start = pl.multiple_of(owner * half + place * size, 64)
            target[at, :] = flat[pl.ds(start, size), :]


def backward_kernel(
    chunk, theirs, ring, taps_one, field_one, taps_mid, field_two, pool, projection, second_kernel,
    mine, other, cot, taps_slope, up, flat,
):
    half_rows, half_cols, wide = theirs.shape
    lanes = projection.shape[0]
    rows, cols, pitch = 2 * half_rows, 2 * half_cols, taps_one.shape[1]
    outs, pitch_two = field_two.shape[:2]
    cot[...] = jnp.zeros(cot.shape, F32)
    cot[1 : half_rows + 1, 0:half_cols] = theirs[...].astype(F32)
    top, bottom = sides(ring[0:cols], ring[cols : 2 * cols], GY)
    at = 2 * cols
    left, right = sides(ring[at : at + EDGE], ring[at + EDGE : at + 2 * EDGE], GX)
    for part in range(2):
        lane = slice(part * lanes, (part + 1) * lanes)
        at = part * half_cols
        cot[0, 0:half_cols, lane] = top[at : at + half_cols]
        cot[half_rows + 1, 0:half_cols, lane] = bottom[at : at + half_cols]
        at = part * (EDGE // 2)
        cot[:, pitch_two - 1 : pitch_two, lane] = left[at : at + outs].reshape(outs, 1, lanes)
        cot[:, half_cols : half_cols + 1, lane] = right[at : at + outs].reshape(outs, 1, lanes)
    slope_two = cot[...] * sloped(field_two[...])
    spread_taps(slope_two, taps_slope, wide)
    own = half_rows * half_cols
    own_slope = slope_two[1 : half_rows + 1, 0:half_cols].reshape(own, wide).astype(BF16)
    windows = [
        taps_mid[row + 1 : row + 1 + half_rows, 0:half_cols].reshape(own, 3 * wide)
        for row in range(3)
    ]
    grad = lax.dot_general(
        jnp.concatenate(windows, axis=1), own_slope, TN, preferred_element_type=F32
    )
    flat[0 : 9 * wide, :] = grad.astype(BF16)
    windows = [
        taps_slope[row : row + half_rows, 0:half_cols].reshape(own, 3 * wide) for row in range(3)
    ]
    kernels = [second_kernel[2 - row, 2 - col] for row in range(3) for col in range(3)]
    kernels = jnp.concatenate(kernels, axis=1)
    windows = jnp.concatenate(windows, axis=1)
    cut = own // 2
    back = [
        lax.dot_general(windows[at : at + cut], kernels, NT, preferred_element_type=F32)
        for at in (0, cut)
    ]
    back = jnp.concatenate(back, axis=0).astype(BF16)
    at = 9 * wide
    flat[at : at + lanes, :] = dot(pool[...].astype(F32).reshape(own, lanes).T.astype(BF16), back).astype(BF16)
    at += lanes
    down = lax.dot_general(back, projection[...], NT, preferred_element_type=F32)
    down = down.astype(BF16).astype(F32) * 0.25
    up[pl.ds(0, own, stride=2), :] = down
    up[pl.ds(1, own, stride=2), :] = down
    cells = 2 * own
    field = field_one[2 : half_rows + 2, 0:cols].reshape(cells, 2 * lanes)
    slope_one = jnp.concatenate([up[...], up[...]], axis=1) * sloped(field)
    slope_one = slope_one.astype(BF16)
    grads = []
    for row in range(4):
        start = REACH - 1 + row
        window = taps_one[start : start + rows].reshape(half_rows, 2, pitch, 3 * lanes)[:, 0, 0:cols]
        window = window.reshape(cells, 3 * lanes)
        grads.append(lax.dot_general(window, slope_one, TN, preferred_element_type=F32))
    for tap in range(9):
        row, col = tap // 3, tap % 3
        span = slice(col * lanes, (col + 1) * lanes)
        grad = grads[row][span, :lanes] + grads[row + 1][span, lanes:]
        top = at + (tap % 4) * lanes + (4 * lanes if tap == 8 else 0)
        side = lanes if 4 <= tap < 8 else 0
        flat[top : top + lanes, side : side + lanes] = grad.astype(BF16)
    top = at + 4 * lanes
    flat[top : top + lanes, lanes : 2 * lanes] = jnp.zeros((lanes, lanes), BF16)
    used = at + 5 * lanes
    total = flat.shape[0]
    if used < total:
        flat[used:total, :] = jnp.zeros((total - used, wide), BF16)
    split_halves(flat, mine, other, chunk)


def resident(*arrays):
    return [pltpu.with_memory_space_constraint(array, pltpu.VMEM) for array in arrays]


def forward(tile, halo, first_kernel, projection, second_kernel):
    rows, cols, lanes = tile.shape
    half_rows, half_cols, wide = rows // 2, cols // 2, projection.shape[1]
    pitch = cols + 2 * SIDE
    pitch_two = pitch // 2
    vmem = pl.BlockSpec(memory_space=pltpu.VMEM)
    return pl.pallas_call(
        forward_kernel,
        out_shape=(
            pltpu.VMEM((half_rows, half_cols, wide), BF16),
            pltpu.VMEM((rows + 2 * REACH, pitch, 3 * lanes), BF16),
            pltpu.VMEM((half_rows + 4, pitch, 2 * lanes), F32),
            pltpu.VMEM((half_rows + 4, pitch_two, 3 * wide), BF16),
            pltpu.VMEM((half_rows + 2, pitch_two, wide), F32),
            pltpu.VMEM((half_rows, half_cols, lanes), BF16),
        ),
        in_specs=[vmem] * 8,
        out_specs=(vmem,) * 6,
        scratch_shapes=[
            pltpu.VMEM((12 * lanes, 2 * lanes), BF16),
            pltpu.VMEM(((half_rows + 4) * pitch, lanes), F32),
        ],
        compiler_params=pltpu.CompilerParams(vmem_limit_bytes=20 << 20),
    )(
        *resident(tile, *halo, first_kernel, projection, second_kernel),
    )


def backward(theirs, ring, kept, projection, second_kernel, total, chunk):
    half_rows, half_cols, wide = theirs.shape
    outs, pitch_two = kept[3].shape[:2]
    lanes = projection.shape[0]
    vmem = pl.BlockSpec(memory_space=pltpu.VMEM)
    return pl.pallas_call(
        functools.partial(backward_kernel, chunk),
        out_shape=(
            pltpu.VMEM((total // 2, wide), BF16),
            pltpu.VMEM((total // 2, wide), BF16),
        ),
        in_specs=[vmem] * 9,
        out_specs=(vmem,) * 2,
        scratch_shapes=[
            pltpu.VMEM((outs, pitch_two, wide), F32),
            pltpu.VMEM((outs, pitch_two, 3 * wide), BF16),
            pltpu.VMEM((4 * half_rows * half_cols // 2, lanes), F32),
            pltpu.VMEM((total, wide), BF16),
        ],
        compiler_params=pltpu.CompilerParams(vmem_limit_bytes=24 << 20),
    )(*resident(theirs, ring, *kept, projection, second_kernel))


def unpack_half(own, chunk, source, grads, held, sent):
    first, projection, second = grads
    lanes, wide = projection.shape
    half, flip = source.shape[0], lax.axis_index(GX[0])
    low = lax.axis_index("core") == (0 if own else 1)
    piece = math.gcd(64, chunk) if chunk else lanes
    jobs = []

    def send(rows, side, target):
        at, inside = rows[0] % half, rows[0] < half
        slot = sent.at[len(jobs)]
        span = slice(at, at + rows[1])
        here = low if inside else jnp.logical_not(low)

        @pl.when(here)
        def _():
            for step in range(at, at + rows[1], piece):
                start = step
                if chunk:
                    start = step + flip * (1 - 2 * (step // chunk % 2)) * chunk
                    start = pl.multiple_of(start, piece)
                held[step : step + piece, side] = source[pl.ds(start, piece), side].astype(F32)
            pltpu.make_async_copy(held.at[span, side], target, slot).start()

        jobs.append((here, held.at[span, side], target, slot))

    whole = slice(0, wide)
    for tap in range(9):
        send((tap * wide, wide), whole, second.at[tap // 3, tap % 3])
    at = 9 * wide
    send((at, lanes), whole, projection)
    at += lanes
    for tap in range(9):
        top = at + (tap % 4) * lanes + (4 * lanes if tap == 8 else 0)
        side = lanes if 4 <= tap < 8 else 0
        send((top, lanes), slice(side, side + lanes), first.at[tap // 3, tap % 3])
    for here, origin, target, slot in jobs:

        @pl.when(here)
        def _(origin=origin, target=target, slot=slot):
            pltpu.make_async_copy(origin, target, slot).wait()


def unpack_own(chunk, source, first, projection, second, held, sent):
    unpack_half(True, chunk, source, (first, projection, second), held, sent)


def unpack_other(
    chunk, source, features, first_in, projection_in, second_in, output, first, projection, second,
    held, sent,
):
    copy = pltpu.make_async_copy(features, output, sent.at[19])
    copy.start()
    unpack_half(False, chunk, source, (first, projection, second), held, sent)
    copy.wait()


def unpack_call(kernel, chunk, arrays, outs, aliases):
    vmem, hbm = pl.BlockSpec(memory_space=pltpu.VMEM), pl.BlockSpec(memory_space=pl.ANY)
    resting = len(aliases)
    moving = resident(*arrays[: len(arrays) - resting])
    return pl.pallas_call(
        functools.partial(kernel, chunk),
        out_shape=outs,
        in_specs=[vmem] * len(moving) + [hbm] * resting,
        out_specs=(hbm,) * len(outs),
        scratch_shapes=[
            pltpu.VMEM(arrays[0].shape, F32),
            pltpu.SemaphoreType.DMA((20,)),
        ],
        input_output_aliases=aliases,
        compiler_params=pltpu.CompilerParams(vmem_limit_bytes=12 << 20),
    )(*moving, *arrays[len(arrays) - resting :])


def swap_pairs(block, axis):
    return lax.ppermute(block, axis, [(0, 1), (1, 0)])


def swap_neighbours(even, odd, axes, spare):
    size, others = lax.axis_size(axes), lax.axis_size(spare)
    near = [(i, i + 1) for i in range(0, size, 2)]
    far = [(i, i + 1) for i in range(1, size - 1, 2)]
    leading = spare == "gy_hi"

    def place(i, at):
        return at * size + i if leading else i * others + at

    far = [(place(i, at), place(j, at)) for i, j in far for at in range(others)]
    ends = [(i, at) for i in (0, size - 1) for at in range(0, others, 2)]
    far += [(place(i, at), place(i, at + 1)) for i, at in ends]
    names = (spare,) + axes if leading else axes + (spare,)

    def both(pairs):
        return [pair for i, j in pairs for pair in ((i, j), (j, i))]

    odd = lax.ppermute(odd, names, both(far))
    even = lax.ppermute(even, axes, both(near))
    return even, odd


def rows_kernel(image, upstream, rows_even, rows_odd, sent):
    rows, _, lanes = image.shape
    half_rows, half_cols, _ = upstream.shape
    lower = lax.axis_index("core") == 0
    copies = []

    def send(source, target):
        copy = pltpu.make_async_copy(source, target, sent.at[len(copies)])
        copy.start()
        copies.append(copy)

    for target, at_end in ((rows_odd, ~lower), (rows_even, lower)):
        start = jnp.where(at_end, rows - REACH, 0)
        row = jnp.where(at_end, half_rows - 1, 0)
        send(image.at[pl.ds(start, REACH)], target.at[0:REACH])
        for part in range(2):
            send(
                upstream.at[row, :, part * lanes : (part + 1) * lanes],
                target.at[REACH, part * half_cols : (part + 1) * half_cols],
            )
    for copy in copies:
        copy.wait()


def strips_kernel(image, upstream, tile_even, tile_odd, strip_even, strip_odd, sent):
    _, cols, _ = image.shape
    _, half_cols, _ = upstream.shape
    left = lax.axis_index("gx_lo") == 0
    copies = []

    def send(source, target):
        copy = pltpu.make_async_copy(source, target, sent.at[len(copies)])
        copy.start()
        copies.append(copy)

    for target, strip, at_end in ((tile_odd, strip_odd, ~left), (tile_even, strip_even, left)):
        start = pl.multiple_of(jnp.where(at_end, cols - SIDE, 0), SIDE)
        cell = pl.multiple_of(jnp.where(at_end, half_cols - SIDE, 0), SIDE)
        send(image.at[:, pl.ds(start, SIDE)], target)
        send(upstream.at[:, pl.ds(cell, SIDE)], strip)
    for copy in copies:
        copy.wait()


def cut(kernel, shapes, image, upstream):
    hbm, vmem = pl.BlockSpec(memory_space=pl.ANY), pl.BlockSpec(memory_space=pltpu.VMEM)
    return pl.pallas_call(
        kernel,
        out_shape=[pltpu.VMEM(shape, BF16) for shape in shapes for _ in range(2)],
        in_specs=[hbm, hbm],
        out_specs=[vmem] * (2 * len(shapes)),
        scratch_shapes=[pltpu.SemaphoreType.DMA((6,))],
        compiler_params=pltpu.CompilerParams(vmem_limit_bytes=4 << 20),
    )(*[pltpu.with_memory_space_constraint(array, pltpu.HBM) for array in (image, upstream)])


def columns_kernel(
    rows_even, rows_odd, tile_even, tile_odd, strip_even, strip_odd, even, odd, edge
):
    rows, side, lanes = tile_even.shape
    half_rows = strip_even.shape[0]
    cols = rows_even.shape[1]
    half_cols = cols // 2
    tall = rows + 2 * REACH
    left = lax.axis_index("gx_lo") == 0
    above, below = sides(rows_even[...], rows_odd[...], GY)
    for target, tile, strip, at_end in (
        (odd, tile_odd, strip_odd, ~left), (even, tile_even, strip_even, left),
    ):

        def near(block):
            return jnp.where(at_end, block[0:REACH, cols - side :], block[0:REACH, 0:side])

        body = jnp.concatenate([near(above), tile[...].astype(F32), near(below)], axis=0)
        target[0 : tall * side] = body.reshape(tall * side, lanes).astype(BF16)
        edge[...] = jnp.zeros(edge.shape, F32)
        cells = strip[...].astype(F32)
        cells = jnp.where(at_end, cells[:, side - 1], cells[:, 0])
        for part in range(2):
            at, first = part * (EDGE // 2), part * half_cols

            def corner(block):
                last = first + half_cols - 1
                low, high = block[REACH, first : first + 1], block[REACH, last : last + 1]
                return jnp.where(at_end, high, low)

            edge[at : at + 1] = corner(above)
            edge[at + 1 : at + half_rows + 1] = cells[:, part * lanes : (part + 1) * lanes]
            at += half_rows + 1
            edge[at : at + 1] = corner(below)
        target[tall * side : tall * side + EDGE] = edge[...].astype(BF16)


def fetch_kernel(*refs):
    count = len(refs) // 2
    sent = refs[-1]
    copies = [pltpu.make_async_copy(refs[i], refs[count + i], sent.at[i]) for i in range(count)]
    for copy in copies:
        copy.start()
    for copy in copies:
        copy.wait()


def fetch(*arrays):
    hbm, vmem = pl.BlockSpec(memory_space=pl.ANY), pl.BlockSpec(memory_space=pltpu.VMEM)
    return pl.pallas_call(
        fetch_kernel,
        out_shape=[pltpu.VMEM(array.shape, array.dtype) for array in arrays],
        in_specs=[hbm] * len(arrays),
        out_specs=[vmem] * len(arrays),
        scratch_shapes=[pltpu.SemaphoreType.DMA((len(arrays),))],
        compiler_params=pltpu.CompilerParams(vmem_limit_bytes=1 << 20),
    )(*[pltpu.with_memory_space_constraint(array, pltpu.HBM) for array in arrays])


def edge_columns(*arrays):
    vmem = pl.BlockSpec(memory_space=pltpu.VMEM)
    rows, side, lanes = arrays[2].shape
    shape = ((rows + 2 * REACH) * side + EDGE, lanes)
    return pl.pallas_call(
        columns_kernel,
        out_shape=(pltpu.VMEM(shape, BF16),) * 2,
        in_specs=[vmem] * 6,
        out_specs=(vmem,) * 2,
        scratch_shapes=[pltpu.VMEM((EDGE, lanes), F32)],
        compiler_params=pltpu.CompilerParams(vmem_limit_bytes=8 << 20),
    )(*resident(*arrays))


def scatter_sum(parts, axes):
    parts = lax.all_to_all(parts, axes, 0, 0, tiled=True)
    return parts.astype(F32).sum(axis=0).astype(BF16)


def gather(part, axes, count):
    parts = jnp.broadcast_to(part[None], (count,) + part.shape)
    return lax.all_to_all(parts, axes, 0, 0, tiled=True).reshape(-1, part.shape[1])


def per_device(images, first_kernel, projection, second_kernel, cotangent):
    image, upstream = images[0], cotangent[0]
    half_rows, _, wide = upstream.shape
    rows, cols, lanes = image.shape
    rows_even, rows_odd = cut(rows_kernel, [(REACH + 1, cols, lanes)], image, upstream)
    shapes = [(rows, SIDE, lanes), (half_rows, SIDE, wide)]
    strips = cut(strips_kernel, shapes, image, upstream)
    rows_even, rows_odd = swap_neighbours(rows_even, rows_odd, GY, "gx_lo")
    packed = edge_columns(rows_even, rows_odd, *strips)
    cols_even, cols_odd = swap_neighbours(*packed, GX, "gy_hi")
    tile, *weights = fetch(image, first_kernel, projection, second_kernel)
    theirs = swap_pairs(upstream, "section")
    ring = [rows_even[REACH], rows_odd[REACH], cols_even[-EDGE:], cols_odd[-EDGE:]]
    ring = swap_pairs(jnp.concatenate(ring), "section")

    planes = lax.axis_size("section") * lax.axis_size("gy_hi") * lax.axis_size("gx_lo")
    lines = lax.axis_size("gx_hi")
    unit = 2 * planes * lines * 16
    total = -(-(9 * wide + 6 * lanes) // unit) * unit
    halo = (rows_even, rows_odd, cols_even, cols_odd)
    output, *kept = forward(tile, halo, *weights)
    output = swap_pairs(output, "section")
    chunk = total // 2 // planes if lines == 2 else 0
    mine, other = backward(theirs, ring, kept, *weights[1:], total, chunk)
    part = (mine.astype(F32) + swap_pairs(other, "core").astype(F32)).astype(BF16)
    part = scatter_sum(part.reshape(planes, -1, wide), PLANE)
    if lines == 2:
        pairs = [(0, 3), (1, 2), (2, 1), (3, 0)]
        theirs = lax.ppermute(part, GX, pairs)
        part = (part.astype(F32) + theirs.astype(F32)).astype(BF16)
    elif lines > 2:
        part = scatter_sum(part.reshape(lines, -1, wide), "gx_hi")
        part = gather(part, "gx_hi", lines)
    whole = gather(part, PLANE, planes)
    others = swap_pairs(whole, "core")
    shapes = (first_kernel.shape, projection.shape, second_kernel.shape)
    outs = tuple(jax.ShapeDtypeStruct(shape, F32) for shape in shapes)
    grads = unpack_call(unpack_own, chunk, (whole,), outs, {})
    outs = (jax.ShapeDtypeStruct(output.shape, BF16),) + outs
    output, *grads = unpack_call(
        unpack_other, chunk, (others, output, *grads), outs, {2: 1, 3: 2, 4: 3}
    )
    return (output[None], *grads)


def solution(mesh):
    shape = dict(mesh.shape)
    sizes = (shape["section"], shape["gy"] // 2, 2, shape["gx"] // 2, 2)
    names = ("section", "gy_hi", "core", "gx_hi", "gx_lo")
    split = jax.sharding.Mesh(mesh.devices.reshape(sizes), names)
    tiles = P("section", GY, GX, None)
    return jax.shard_map(
        per_device,
        mesh=split,
        in_specs=(tiles, P(), P(), P(), tiles),
        out_specs=(tiles, P(), P(), P()),
        check_vma=False,
    )
```
